32 devices in a mesh: row: 4 (over z), col: 8 (over y, x, core).
Axes of the slice: x: 2, y: 2, z: 4, core: 2. Of those that a mesh axis runs over, the one named last changes fastest.
Arguments:
- tokens: bfloat16 [512, 8192], P('col', 'row'), may hold values from -6 to 6
- modality: int32 [512], P('row'), may hold values 0 or 1
- in_weight: bfloat16 [8192, 2, 28672], P('row', None, 'col'), may hold values from -0.0625 to 0.0625
- down_weight: bfloat16 [28672, 8192], P('col', 'row'), may hold values from -0.03125 to 0.03125
- d_mixed: bfloat16 [512, 8192], P('col', 'row'), may hold values from -6 to 6
Outputs:
- mixed: bfloat16 [512, 8192], P('col', 'row')
- d_down: bfloat16 [28672, 8192], P('col', 'row')
- d_in: bfloat16 [8192, 2, 28672], P('row', None, 'col')
- d_tokens: bfloat16 [512, 8192], P('col', 'row')
The draws below stay inside these ranges and needn't reach their ends.
All inputs are finite; a program needn't handle non-finite values. No bound on the sum of `modality` on one device may be relied on, other than what follows from the above.
Results may differ from the reference program's by a relative error of at most 0.0049.
Values may be sent and summed in bfloat16 or wider, within the bound.
A program may use at most 192 MiB of HBM per device.

```python
import jax
import jax.numpy as jnp

D = 8192
FF = 28672
TOKENS = 512


def touch_ends(result, rng, least, top_value):
    index_at = [jax.random.randint(jax.random.fold_in(rng, axis), (), 0, length) for axis, length in enumerate(result.shape)]
    longest = result.shape.index(max(result.shape))
    next_to = index_at[:longest] + [(index_at[longest] + 1) % result.shape[longest]] + index_at[longest + 1:]
    return result.at[tuple(index_at)].set(least).at[tuple(next_to)].set(top_value)


def block_levels(key, shape, cuts, low, high):
    factor_of, own = 1.0, jax.random.fold_in(key, 6)
    for position, shards_of in cuts:
        steps = jnp.exp(jax.random.uniform(jax.random.fold_in(own, position), (shards_of,), jnp.float32, low / len(cuts), high / len(cuts)))
        factor_of = factor_of * jnp.repeat(steps, shape[position] // shards_of).reshape([-1 if axis == position else 1 for axis in range(len(shape))])
    return factor_of


def noise(key, shape, scale, bound, split=(), held_as=jnp.bfloat16):
    drawn = scale * jax.random.normal(key, shape, jnp.float32)
    if split:
        drawn = drawn * block_levels(key, shape, split, -0.22, 0.18)
    return jnp.clip(drawn, -bound, bound).astype(held_as)


def setup_inputs(seed: int = 0) -> dict:
    key_of = jax.random.split(jax.random.key(seed), 6)
    tokens = noise(key_of[0], (TOKENS, D), 1.0, 6.0, ((0, 8), (1, 4)))
    modality = touch_ends((jax.random.randint(key_of[1], (TOKENS,), 0, 2) < 1).astype(jnp.int32), jax.random.fold_in(key_of[1], 1), 0, 1)
    in_weight = noise(key_of[2], (D, 2, FF), D ** -0.5, 0.0625, ((0, 4), (2, 8)))
    down_weight = noise(key_of[3], (FF, D), FF ** -0.5, 0.03125, ((0, 8), (1, 4)))
    d_mixed = noise(key_of[4], (TOKENS, D), 1.0, 6.0, ((0, 8), (1, 4)))
    return {"tokens": tokens, "modality": modality, "in_weight": in_weight, "down_weight": down_weight, "d_mixed": d_mixed}


def reference(tokens, modality, in_weight, down_weight, d_mixed):
    selected = (modality == 1).astype(jnp.float32)[:, None]
    flat_in = in_weight.reshape(D, 2 * FF)
    projected = jnp.dot(tokens, flat_in, preferred_element_type=jnp.float32)
    gate_part = projected[:, :FF]
    up_part = projected[:, FF:]
    sigmoid_gate = jax.nn.sigmoid(gate_part)
    activated = gate_part * sigmoid_gate
    hidden = (selected * activated * up_part).astype(jnp.bfloat16)
    mixed = jnp.dot(hidden, down_weight, preferred_element_type=jnp.float32).astype(jnp.bfloat16)
    d_down = jnp.dot(hidden.T, d_mixed, preferred_element_type=jnp.float32).astype(jnp.bfloat16)
    d_hidden = jnp.dot(d_mixed, down_weight.T, preferred_element_type=jnp.float32)
    d_scaled = selected * d_hidden
    d_gate = d_scaled * up_part * (sigmoid_gate + gate_part * sigmoid_gate * (1.0 - sigmoid_gate))
    d_up = d_scaled * activated
    d_projected = jnp.concatenate([d_gate, d_up], 1).astype(jnp.bfloat16)
    d_in = jnp.dot(tokens.T, d_projected, preferred_element_type=jnp.float32).reshape(D, 2, FF).astype(jnp.bfloat16)
    d_tokens = jnp.dot(d_projected, flat_in.T, preferred_element_type=jnp.float32).astype(jnp.bfloat16)
    return mixed, d_down, d_in, d_tokens
```

```python
import functools

import jax
import jax.numpy as jnp
from jax import lax
from jax.experimental import pallas as pl
from jax.experimental.pallas import tpu as pltpu
from jax.sharding import PartitionSpec as P

MESH = pl.DeviceIdType.MESH
OVER_LAST = (((1,), (1,)), ((), ()))
OVER_FIRST = (((0,), (0,)), ((), ()))


def dot(a, b, dims=(((1,), (0,)), ((), ()))):
    return lax.dot_general(a, b, dims, preferred_element_type=jnp.float32)


def exchange(partial, axis):
    count = lax.axis_size(axis)
    me = lax.axis_index(axis)
    rows = partial.shape[0] // count
    received = []
    for shift in range(1, count):
        start = lax.rem(me + shift, count) * rows
        block = lax.dynamic_slice_in_dim(partial, start, rows, 0).astype(jnp.bfloat16)
        moves = [(i, (i + shift) % count) for i in range(count)]
        received.append(lax.ppermute(block, axis, moves))
    total = lax.dynamic_slice_in_dim(partial, me * rows, rows, 0)
    for block in received:
        total = total + block.astype(jnp.float32)
    return total


def paired_columns(rows_ref, gate_ref, up_ref, out_ref):
    for part, side_ref in enumerate((gate_ref, up_ref)):
        out_ref[:, part, :] = dot(rows_ref[...], side_ref[...], OVER_FIRST).astype(jnp.bfloat16)


def in_gradient(rows, d_projected):
    count, depth = rows.shape
    width = d_projected.shape[1] // 2
    deep = depth // 8
    wide = max(w for w in range(128, 2049, 128) if width % w == 0)
    return pl.pallas_call(
        paired_columns,
        grid=(width // wide, depth // deep),
        in_specs=[
            pl.BlockSpec((count, deep), lambda j, i: (0, i)),
            pl.BlockSpec((count, wide), lambda j, i: (0, j)),
            pl.BlockSpec((count, wide), lambda j, i: (0, j + width // wide)),
        ],
        out_specs=pl.BlockSpec((deep, 2, wide), lambda j, i: (i, 0, j)),
        out_shape=jax.ShapeDtypeStruct((depth, 2, width), jnp.bfloat16),
        cost_estimate=pl.CostEstimate(
            flops=4 * count * depth * width,
            bytes_accessed=4 * (depth * width + count * width + count * depth),
            transcendentals=0,
        ),
    )(rows, d_projected, d_projected)


def swiglu_terms(gate, up, d_hidden):
    sig = jax.nn.sigmoid(gate)
    activated = gate * sig
    d_gate = d_hidden * up * (sig + gate * sig * (1.0 - sig))
    return activated * up, d_gate, d_hidden * activated


def block_terms(rows, cotangents, in_weight, down_weight):
    width = in_weight.shape[2]
    flat_in = in_weight.reshape(in_weight.shape[0], -1)
    d_hidden = exchange(dot(cotangents, down_weight, OVER_LAST), "row")
    projected = exchange(dot(rows, flat_in), "row")
    hidden, d_gate, d_up = swiglu_terms(projected[:, :width], projected[:, width:], d_hidden)
    d_local = jnp.concatenate([d_gate, d_up], 1).astype(jnp.bfloat16)
    hidden_all = lax.all_gather(hidden.astype(jnp.bfloat16), "row", axis=0, tiled=True)
    d_projected = lax.all_gather(d_local, "row", axis=0, tiled=True)
    mixed = exchange(dot(hidden_all, down_weight), "col").astype(jnp.bfloat16)
    d_down = dot(hidden_all, cotangents, OVER_FIRST).astype(jnp.bfloat16)
    d_tokens = exchange(dot(d_projected, flat_in, OVER_LAST), "col").astype(jnp.bfloat16)
    return (mixed, d_down, in_gradient(rows, d_projected), d_tokens)


def chain_kernel(
    size, units, wide, rows_ref, cots_ref, in_ref, down_ref, mixed_ref, d_tokens_ref, terms_ref,
    raw, w_down, w_in, partial, sums, terms,
    load_sem, sum_send, sum_recv, term_send, term_recv, out_sem,
):
    z = lax.axis_index("row")
    middle = size // 2
    slots = w_down.shape[0]
    held = partial.shape[0]
    near = jnp.minimum(z, size - 1 - z)
    last_lag = 2 * middle + 1 - near

    def owner_of(u):
        return middle - 1 + lax.rem(u, 2)

    def loads(u):
        columns = pl.ds(pl.multiple_of(u * wide, wide), wide)
        slot = lax.rem(u, 2)
        return (
            pltpu.make_async_copy(in_ref.at[:, :, columns], raw.at[slot], load_sem.at[0, slot]),
            pltpu.make_async_copy(down_ref.at[columns, :], w_down.at[lax.rem(u, slots)], load_sem.at[1, slot]),
        )

    def sum_copy(u, side):
        return pltpu.make_async_remote_copy(
            src_ref=sums.at[side, u], dst_ref=sums.at[side, u],
            send_sem=sum_send.at[u], recv_sem=sum_recv.at[side, u],
            device_id={"row": z + 1 - 2 * side}, device_id_type=MESH,
        )

    def term_copy(u, side):
        return pltpu.make_async_remote_copy(
            src_ref=terms.at[u], dst_ref=terms.at[u],
            send_sem=term_send.at[side, u], recv_sem=term_recv.at[u],
            device_id={"row": z + 1 - 2 * side}, device_id_type=MESH,
        )

    def out_copy(u):
        columns = pl.ds(pl.multiple_of(u * 3 * wide, wide), 3 * wide)
        return pltpu.make_async_copy(terms.at[u], terms_ref.at[:, columns], out_sem.at[u])

    barrier = pltpu.get_barrier_semaphore()
    for step in (-1, 1):
        @pl.when((z + step >= 0) & (z + step < size))
        def _():
            pl.semaphore_signal(barrier, inc=1, device_id={"row": z + step}, device_id_type=MESH)
    for copy in loads(0):
        copy.start()
    mixed_ref[...] = jnp.zeros_like(mixed_ref)
    d_tokens_ref[...] = jnp.zeros_like(d_tokens_ref)
    pl.semaphore_wait(barrier, jnp.where(near > 0, 2, 1))

    @pl.loop(0, units + 2 * middle + 1)
    def _(t):
        @pl.when(t < units)
        def _():
            for copy in loads(t):
                copy.wait()

            @pl.when(t + 1 < units)
            def _():
                for copy in loads(t + 1):
                    copy.start()

            slot, here = lax.rem(t, slots), lax.rem(t, held)
            for part in range(2):
                w_in[slot, :, part * wide:(part + 1) * wide] = raw[lax.rem(t, 2), :, part, :]
            partial[here, :, :2 * wide] = dot(rows_ref[...], w_in[slot])
            partial[here, :, 2 * wide:] = dot(cots_ref[...], w_down[slot], OVER_LAST)

        relayed = t - near

        @pl.when((relayed >= 0) & (relayed < units) & (owner_of(relayed) != z))
        def _():
            side = jnp.where(z < owner_of(relayed), 0, 1)
            here = lax.rem(relayed, held)

            @pl.when(near > 0)
            def _():
                sum_copy(relayed, side).wait_recv()
                sums[side, relayed] = (
                    partial[here] + sums[side, relayed].astype(jnp.float32)
                ).astype(sums.dtype)

            @pl.when(near == 0)
            def _():
                sums[side, relayed] = partial[here].astype(sums.dtype)

            sum_copy(relayed, side).start()

        closed = t - middle

        @pl.when((closed >= 0) & (closed < units) & (owner_of(closed) == z))
        def _():
            here = lax.rem(closed, held)

            @pl.when(z > 0)
            def _():
                sum_copy(closed, 0).wait_recv()
                partial[here] += sums[0, closed].astype(jnp.float32)

            @pl.when(z < size - 1)
            def _():
                sum_copy(closed, 1).wait_recv()
                partial[here] += sums[1, closed].astype(jnp.float32)

            whole = partial[here]
            results = swiglu_terms(*(whole[:, k * wide:(k + 1) * wide] for k in range(3)))
            for k, result in enumerate(results):
                terms[closed, :, k * wide:(k + 1) * wide] = result.astype(jnp.bfloat16)

            @pl.when(z < size - 1)
            def _():
                term_copy(closed, 0).start()

            @pl.when(z > 0)
            def _():
                term_copy(closed, 1).start()

        used = t - last_lag

        @pl.when((used >= 0) & (used < units))
        def _():
            owner = owner_of(used)

            @pl.when(owner != z)
            def _():
                side = jnp.where(z < owner, 1, 0)
                term_copy(used, side).wait_recv()

                @pl.when(near > 0)
                def _():
                    term_copy(used, side).start()

            out_copy(used).start()
            slot = lax.rem(used, slots)
            mixed_ref[...] += dot(terms[used, :, :wide], w_down[slot])
            d_tokens_ref[...] += dot(terms[used, :, wide:], w_in[slot], OVER_LAST)

    @pl.loop(0, units)
    def _(u):
        owner = owner_of(u)
        out_copy(u).wait()

        @pl.when(owner != z)
        def _():
            sum_copy(u, jnp.where(z < owner, 0, 1)).wait_send()

            @pl.when(near > 0)
            def _():
                term_copy(u, jnp.where(z < owner, 1, 0)).wait_send()

        @pl.when(owner == z)
        def _():
            @pl.when(z < size - 1)
            def _():
                term_copy(u, 0).wait_send()

            @pl.when(z > 0)
            def _():
                term_copy(u, 1).wait_send()


def chain(rows, cotangents, in_weight, down_weight, collective_id):
    size = lax.axis_size("row")
    count, depth = rows.shape
    width = down_weight.shape[0]
    wide = 128
    units = width // wide
    slots = 2 * (size // 2) + 4
    held = size // 2 + 1
    sum_type = jnp.bfloat16 if size <= 4 else jnp.float32
    vmem, hbm = pl.BlockSpec(memory_space=pltpu.VMEM), pl.BlockSpec(memory_space=pl.ANY)
    dma = pltpu.SemaphoreType.DMA
    return pl.pallas_call(
        functools.partial(chain_kernel, size, units, wide),
        in_specs=[vmem, vmem, hbm, hbm],
        out_specs=[vmem, vmem, hbm],
        out_shape=[
            jax.ShapeDtypeStruct((count, depth), jnp.float32),
            jax.ShapeDtypeStruct((count, depth), jnp.float32),
            jax.ShapeDtypeStruct((count, 3 * width), jnp.bfloat16),
        ],
        scratch_shapes=[
            pltpu.VMEM((2, depth, 2, wide), jnp.bfloat16),
            pltpu.VMEM((slots, wide, depth), jnp.bfloat16),
            pltpu.VMEM((slots, depth, 2 * wide), jnp.bfloat16),
            pltpu.VMEM((held, count, 3 * wide), jnp.float32),
            pltpu.VMEM((2, units, count, 3 * wide), sum_type),
            pltpu.VMEM((units, count, 3 * wide), jnp.bfloat16),
            dma((2, 2)), dma((units,)), dma((2, units)), dma((2, units)), dma((units,)), dma((units,)),
        ],
        compiler_params=pltpu.CompilerParams(
            collective_id=collective_id, has_side_effects=True, vmem_limit_bytes=60 * 1024 * 1024
        ),
        cost_estimate=pl.CostEstimate(
            flops=12 * count * depth * width, bytes_accessed=6 * depth * width, transcendentals=count * width
        ),
    )(rows, cotangents, in_weight, down_weight)


def weight_kernel(group, wide, rows_ref, cots_ref, terms_ref, d_in_ref, d_down_ref):
    for g in range(group):
        columns = slice(g * wide, (g + 1) * wide)
        base = 3 * g * wide
        d_down_ref[columns, :] = dot(
            terms_ref[:, base:base + wide], cots_ref[...], OVER_FIRST
        ).astype(jnp.bfloat16)
        both = dot(rows_ref[...], terms_ref[:, base + wide:base + 3 * wide], OVER_FIRST).astype(jnp.bfloat16)
        for part in range(2):
            d_in_ref[:, part, columns] = both[:, part * wide:(part + 1) * wide]


def weight_gradients(rows, cotangents, terms):
    count, depth = rows.shape
    wide = 128
    width = terms.shape[1] // 3
    units = width // wide
    group = 2 if units % 2 == 0 else 1
    return pl.pallas_call(
        functools.partial(weight_kernel, group, wide),
        grid=(units // group,),
        in_specs=[
            pl.BlockSpec((count, depth), lambda j: (0, 0)),
            pl.BlockSpec((count, depth), lambda j: (0, 0)),
            pl.BlockSpec((count, 3 * group * wide), lambda j: (0, j)),
        ],
        out_specs=[
            pl.BlockSpec((depth, 2, group * wide), lambda j: (0, 0, j)),
            pl.BlockSpec((group * wide, depth), lambda j: (j, 0)),
        ],
        out_shape=[
            jax.ShapeDtypeStruct((depth, 2, width), jnp.bfloat16),
            jax.ShapeDtypeStruct((width, depth), jnp.bfloat16),
        ],
        cost_estimate=pl.CostEstimate(
            flops=6 * count * depth * width,
            bytes_accessed=6 * depth * width + 6 * count * width + 4 * count * depth,
            transcendentals=0,
        ),
    )(rows, cotangents, terms)


def per_device(tokens, modality, in_weight, down_weight, d_mixed):
    every = lambda x: lax.all_gather(x, "col", axis=0, tiled=True)
    rows_all = every(tokens)
    cots_all = every(d_mixed)
    chosen = lax.all_gather(modality, "row", axis=0, tiled=True) == 1
    total = chosen.shape[0]
    place = jnp.cumsum(chosen.astype(jnp.int32)) - 1
    packed = total * 9 // 16

    def packed_form(rows, cotangents, w_in, w_down):
        pick = (chosen[None, :] & (place[None, :] == jnp.arange(packed)[:, None])).astype(jnp.bfloat16)
        take = lambda x: dot(pick, x).astype(jnp.bfloat16)
        spread = lambda x: dot(pick, x.astype(jnp.bfloat16), OVER_FIRST)
        rows, cotangents = take(rows), take(cotangents)
        mixed, d_tokens, terms = chain(rows, cotangents, w_in, w_down, 1)
        d_in, d_down = weight_gradients(rows, cotangents, terms)
        mixed = exchange(spread(mixed), "col").astype(jnp.bfloat16)
        d_tokens = exchange(spread(d_tokens), "col").astype(jnp.bfloat16)
        return (mixed, d_down, d_in, d_tokens)

    def whole_form(rows, cotangents, w_in, w_down):
        keep = chosen[:, None].astype(jnp.bfloat16)
        return block_terms(rows * keep, cotangents * keep, w_in, w_down)

    return lax.cond(
        place[-1] < packed, packed_form, whole_form, rows_all, cots_all, in_weight, down_weight
    )


def solution(mesh):
    return jax.shard_map(
        per_device,
        mesh=mesh,
        in_specs=(
            P("col", "row"),
            P("row"),
            P("row", None, "col"),
            P("col", "row"),
            P("col", "row"),
        ),
        out_specs=(P("col", "row"), P("col", "row"), P("row", None, "col"), P("col", "row")),
        check_vma=False,
    )
```

```python
import functools

import jax
import jax.numpy as jnp
from jax import lax
from jax.experimental import pallas as pl
from jax.experimental.pallas import tpu as pltpu
from jax.sharding import PartitionSpec as P

MESH = pl.DeviceIdType.MESH
OVER_LAST = (((1,), (1,)), ((), ()))
OVER_FIRST = (((0,), (0,)), ((), ()))


def dot(a, b, dims=(((1,), (0,)), ((), ()))):
    return lax.dot_general(a, b, dims, preferred_element_type=jnp.float32)


def exchange(partial, axis):
    count = lax.axis_size(axis)
    me = lax.axis_index(axis)
    rows = partial.shape[0] // count
    received = []
    for shift in range(1, count):
        start = lax.rem(me + shift, count) * rows
        block = lax.dynamic_slice_in_dim(partial, start, rows, 0).astype(jnp.bfloat16)
        moves = [(i, (i + shift) % count) for i in range(count)]
        received.append(lax.ppermute(block, axis, moves))
    total = lax.dynamic_slice_in_dim(partial, me * rows, rows, 0)
    for block in received:
        total = total + block.astype(jnp.float32)
    return total


def paired_columns(rows_ref, gate_ref, up_ref, out_ref):
    for part, side_ref in enumerate((gate_ref, up_ref)):
        out_ref[:, part, :] = dot(rows_ref[...], side_ref[...], OVER_FIRST).astype(jnp.bfloat16)


def in_gradient(rows, d_gate, d_up):
    count, depth = rows.shape
    width = d_gate.shape[1]
    deep = depth // 8
    return pl.pallas_call(
        paired_columns,
        grid=(depth // deep,),
        in_specs=[
            pl.BlockSpec((count, deep), lambda i: (0, i)),
            pl.BlockSpec((count, width), lambda i: (0, 0)),
            pl.BlockSpec((count, width), lambda i: (0, 0)),
        ],
        out_specs=pl.BlockSpec((deep, 2, width), lambda i: (i, 0, 0)),
        out_shape=jax.ShapeDtypeStruct((depth, 2, width), jnp.bfloat16),
        cost_estimate=pl.CostEstimate(
            flops=4 * count * depth * width,
            bytes_accessed=4 * (depth * width + count * width + count * depth),
            transcendentals=0,
        ),
    )(rows, d_gate, d_up)


def swiglu_terms(gate, up, d_hidden):
    sig = jax.nn.sigmoid(gate)
    activated = gate * sig
    d_gate = d_hidden * up * (sig + gate * sig * (1.0 - sig))
    return activated * up, d_gate, d_hidden * activated


def block_terms(rows, cotangents, in_weight, down_weight):
    width = in_weight.shape[2]
    flat_in = in_weight.reshape(in_weight.shape[0], -1)
    d_hidden = exchange(dot(cotangents, down_weight, OVER_LAST), "row")
    projected = exchange(dot(rows, flat_in), "row")
    hidden, d_gate, d_up = swiglu_terms(projected[:, :width], projected[:, width:], d_hidden)
    d_local = jnp.concatenate([d_gate, d_up], 1).astype(jnp.bfloat16)
    hidden_all = lax.all_gather(hidden.astype(jnp.bfloat16), "row", axis=0, tiled=True)
    d_projected = lax.all_gather(d_local, "row", axis=0, tiled=True)
    mixed = exchange(dot(hidden_all, down_weight), "col").astype(jnp.bfloat16)
    d_down = dot(hidden_all, cotangents, OVER_FIRST).astype(jnp.bfloat16)
    d_tokens = exchange(dot(d_projected, flat_in, OVER_LAST), "col").astype(jnp.bfloat16)
    return (mixed, d_down, in_gradient(rows, d_projected[:, :width], d_projected[:, width:]), d_tokens)


def unpack(pairs_ref, columns_ref, apart):
    depth, _, wide = pairs_ref.shape
    tall = apart.shape[1] // 2
    for step in range(depth // tall):
        rows, buffer = slice(step * tall, (step + 1) * tall), step % apart.shape[0]
        apart[buffer] = pairs_ref[rows].reshape(2 * tall, wide).astype(jnp.float32)
        for part in range(2):
            one = apart[buffer, pl.ds(part, tall, stride=2), :]
            columns_ref[rows, part * wide:(part + 1) * wide] = one.astype(jnp.bfloat16)


def chain_kernel(
    size, units, wide, rows_ref, cots_ref, in_ref, down_ref, total_ref, hidden_ref, d_gate_ref, d_up_ref,
    raw, apart, w_down, w_in, partial, sums, terms,
    load_sem, sum_send, sum_recv, term_send, term_recv, out_sem,
):
    z = lax.axis_index("row")
    middle = size // 2
    slots = w_down.shape[0]
    held = partial.shape[0]
    near = jnp.minimum(z, size - 1 - z)
    last_lag = 2 * middle + 1 - near

    def owner_of(u):
        return middle - 1 + lax.rem(u, 2)

    def loads(u):
        columns = pl.ds(pl.multiple_of(u * wide, wide), wide)
        slot = lax.rem(u, 2)
        return (
            pltpu.make_async_copy(in_ref.at[:, :, columns], raw.at[slot], load_sem.at[0, slot]),
            pltpu.make_async_copy(down_ref.at[columns, :], w_down.at[lax.rem(u, slots)], load_sem.at[1, slot]),
        )

    def sum_copy(u, side):
        return pltpu.make_async_remote_copy(
            src_ref=sums.at[side, u], dst_ref=sums.at[side, u],
            send_sem=sum_send.at[u], recv_sem=sum_recv.at[side, u],
            device_id={"row": z + 1 - 2 * side}, device_id_type=MESH,
        )

    def term_copy(u, side):
        return pltpu.make_async_remote_copy(
            src_ref=terms.at[u], dst_ref=terms.at[u],
            send_sem=term_send.at[side, u], recv_sem=term_recv.at[u],
            device_id={"row": z + 1 - 2 * side}, device_id_type=MESH,
        )

    def out_copies(u):
        columns = pl.ds(pl.multiple_of(u * wide, wide), wide)
        return [
            pltpu.make_async_copy(
                terms.at[u, :, k * wide:(k + 1) * wide], ref.at[:, columns], out_sem.at[k, u]
            )
            for k, ref in enumerate((hidden_ref, d_gate_ref, d_up_ref))
        ]

    barrier = pltpu.get_barrier_semaphore()
    for step in (-1, 1):
        @pl.when((z + step >= 0) & (z + step < size))
        def _():
            pl.semaphore_signal(barrier, inc=1, device_id={"row": z + step}, device_id_type=MESH)
    for copy in loads(0):
        copy.start()
    total_ref[...] = jnp.zeros_like(total_ref)
    depth = down_ref.shape[1]
    pl.semaphore_wait(barrier, jnp.where(near > 0, 2, 1))

    @pl.loop(0, units + 2 * middle + 1)
    def _(t):
        @pl.when(t < units)
        def _():
            for copy in loads(t):
                copy.wait()

            @pl.when(t + 1 < units)
            def _():
                for copy in loads(t + 1):
                    copy.start()

            slot, here = lax.rem(t, slots), lax.rem(t, held)
            unpack(raw.at[lax.rem(t, 2)], w_in.at[slot], apart)
            partial[here, :, :2 * wide] = dot(rows_ref[...], w_in[slot])
            partial[here, :, 2 * wide:] = dot(cots_ref[...], w_down[slot], OVER_LAST)

        relayed = t - near

        @pl.when((relayed >= 0) & (relayed < units) & (owner_of(relayed) != z))
        def _():
            side = jnp.where(z < owner_of(relayed), 0, 1)
            here = lax.rem(relayed, held)

            @pl.when(near > 0)
            def _():
                sum_copy(relayed, side).wait_recv()
                sums[side, relayed] = (
                    partial[here] + sums[side, relayed].astype(jnp.float32)
                ).astype(sums.dtype)

            @pl.when(near == 0)
            def _():
                sums[side, relayed] = partial[here].astype(sums.dtype)

            sum_copy(relayed, side).start()

        closed = t - middle

        @pl.when((closed >= 0) & (closed < units) & (owner_of(closed) == z))
        def _():
            here = lax.rem(closed, held)

            @pl.when(z > 0)
            def _():
                sum_copy(closed, 0).wait_recv()
                partial[here] += sums[0, closed].astype(jnp.float32)

            @pl.when(z < size - 1)
            def _():
                sum_copy(closed, 1).wait_recv()
                partial[here] += sums[1, closed].astype(jnp.float32)

            whole = partial[here]
            results = swiglu_terms(*(whole[:, k * wide:(k + 1) * wide] for k in range(3)))
            for k, result in enumerate(results):
                terms[closed, :, k * wide:(k + 1) * wide] = result.astype(jnp.bfloat16)

            @pl.when(z < size - 1)
            def _():
                term_copy(closed, 0).start()

            @pl.when(z > 0)
            def _():
                term_copy(closed, 1).start()

        used = t - last_lag

        @pl.when((used >= 0) & (used < units))
        def _():
            owner = owner_of(used)

            @pl.when(owner != z)
            def _():
                side = jnp.where(z < owner, 1, 0)
                term_copy(used, side).wait_recv()

                @pl.when(near > 0)
                def _():
                    term_copy(used, side).start()

            for copy in out_copies(used):
                copy.start()
            slot = lax.rem(used, slots)
            total_ref[:, :depth] += dot(terms[used, :, :wide], w_down[slot])
            total_ref[:, depth:] += dot(terms[used, :, wide:], w_in[slot], OVER_LAST)

    @pl.loop(0, units)
    def _(u):
        owner = owner_of(u)
        for copy in out_copies(u):
            copy.wait()

        @pl.when(owner != z)
        def _():
            sum_copy(u, jnp.where(z < owner, 0, 1)).wait_send()

            @pl.when(near > 0)
            def _():
                term_copy(u, jnp.where(z < owner, 1, 0)).wait_send()

        @pl.when(owner == z)
        def _():
            @pl.when(z < size - 1)
            def _():
                term_copy(u, 0).wait_send()

            @pl.when(z > 0)
            def _():
                term_copy(u, 1).wait_send()


def chain(rows, cotangents, in_weight, down_weight, collective_id):
    size = lax.axis_size("row")
    count, depth = rows.shape
    width = down_weight.shape[0]
    wide = 128
    units = width // wide
    slots = 2 * (size // 2) + 4
    held = size // 2 + 1
    sum_type = jnp.bfloat16 if size <= 4 else jnp.float32
    vmem, hbm = pl.BlockSpec(memory_space=pltpu.VMEM), pl.BlockSpec(memory_space=pl.ANY)
    dma = pltpu.SemaphoreType.DMA
    return pl.pallas_call(
        functools.partial(chain_kernel, size, units, wide),
        in_specs=[vmem, vmem, hbm, hbm],
        out_specs=[vmem, hbm, hbm, hbm],
        out_shape=[jax.ShapeDtypeStruct((count, 2 * depth), jnp.float32)]
        + 3 * [jax.ShapeDtypeStruct((count, width), jnp.bfloat16)],
        scratch_shapes=[
            pltpu.VMEM((2, depth, 2, wide), jnp.bfloat16),
            pltpu.VMEM((4, 128, wide), jnp.float32),
            pltpu.VMEM((slots, wide, depth), jnp.bfloat16),
            pltpu.VMEM((slots, depth, 2 * wide), jnp.bfloat16),
            pltpu.VMEM((held, count, 3 * wide), jnp.float32),
            pltpu.VMEM((2, units, count, 3 * wide), sum_type),
            pltpu.VMEM((units, count, 3 * wide), jnp.bfloat16),
            dma((2, 2)), dma((units,)), dma((2, units)), dma((2, units)), dma((units,)), dma((3, units)),
        ],
        compiler_params=pltpu.CompilerParams(
            collective_id=collective_id, has_side_effects=True, vmem_limit_bytes=60 * 1024 * 1024
        ),
        cost_estimate=pl.CostEstimate(
            flops=12 * count * depth * width, bytes_accessed=6 * depth * width, transcendentals=count * width
        ),
    )(rows, cotangents, in_weight, down_weight)


def per_device(tokens, modality, in_weight, down_weight, d_mixed):
    every = lambda x: lax.all_gather(x, "col", axis=0, tiled=True)
    rows_all = every(tokens)
    cots_all = every(d_mixed)
    chosen = lax.all_gather(modality, "row", axis=0, tiled=True) == 1
    total = chosen.shape[0]
    place = jnp.cumsum(chosen.astype(jnp.int32)) - 1
    packed = total * 9 // 16

    def packed_form(rows, cotangents, w_in, w_down):
        pick = (chosen[None, :] & (place[None, :] == jnp.arange(packed)[:, None])).astype(jnp.bfloat16)
        take = lambda x: dot(pick, x).astype(jnp.bfloat16)
        spread = lambda x: dot(pick, x.astype(jnp.bfloat16), OVER_FIRST)
        rows, cotangents = take(rows), take(cotangents)
        depth = rows.shape[1]
        total, hidden, d_gate, d_up = chain(rows, cotangents, w_in, w_down, 1)
        total = exchange(spread(total), "col").astype(jnp.bfloat16)
        d_down = dot(hidden, cotangents, OVER_FIRST).astype(jnp.bfloat16)
        return (total[:, :depth], d_down, in_gradient(rows, d_gate, d_up), total[:, depth:])

    def whole_form(rows, cotangents, w_in, w_down):
        keep = chosen[:, None].astype(jnp.bfloat16)
        return block_terms(rows * keep, cotangents * keep, w_in, w_down)

    return lax.cond(
        place[-1] < packed, packed_form, whole_form, rows_all, cots_all, in_weight, down_weight
    )


def solution(mesh):
    return jax.shard_map(
        per_device,
        mesh=mesh,
        in_specs=(
            P("col", "row"),
            P("row"),
            P("row", None, "col"),
            P("col", "row"),
            P("col", "row"),
        ),
        out_specs=(P("col", "row"), P("col", "row"), P("row", None, "col"), P("col", "row")),
        check_vma=False,
    )
```

```python
import functools
import math

import jax
import jax.numpy as jnp
from jax import lax
from jax.experimental import pallas as pl
from jax.experimental.pallas import tpu as pltpu
from jax.sharding import PartitionSpec as P

MESH = pl.DeviceIdType.MESH
OVER_LAST = (((1,), (1,)), ((), ()))
OVER_FIRST = (((0,), (0,)), ((), ()))


def dot(a, b, dims=(((1,), (0,)), ((), ()))):
    return lax.dot_general(a, b, dims, preferred_element_type=jnp.float32)


def exchange(partial, axis):
    count = lax.axis_size(axis)
    me = lax.axis_index(axis)
    rows = partial.shape[0] // count
    received = []
    for shift in range(1, count):
        start = lax.rem(me + shift, count) * rows
        block = lax.dynamic_slice_in_dim(partial, start, rows, 0).astype(jnp.bfloat16)
        moves = [(i, (i + shift) % count) for i in range(count)]
        received.append(lax.ppermute(block, axis, moves))
    total = lax.dynamic_slice_in_dim(partial, me * rows, rows, 0)
    for block in received:
        total = total + block.astype(jnp.float32)
    return total


def gather(block, axis):
    count = lax.axis_size(axis)
    me = lax.axis_index(axis)
    out = jnp.zeros((count,) + block.shape, block.dtype)
    out = lax.dynamic_update_index_in_dim(out, block, me, 0)
    for shift in range(1, count):
        moves = [(i, (i + shift) % count) for i in range(count)]
        arrived = lax.ppermute(block, axis, moves)
        out = lax.dynamic_update_index_in_dim(out, arrived, lax.rem(me + count - shift, count), 0)
    return out.reshape((count * block.shape[0],) + block.shape[1:])


def paired_columns(rows_ref, gate_ref, up_ref, out_ref):
    for part, side_ref in enumerate((gate_ref, up_ref)):
        out_ref[:, part, :] = dot(rows_ref[...], side_ref[...], OVER_FIRST).astype(jnp.bfloat16)


def in_gradient(packed, d_gate, d_up):
    _, count, depth = packed.shape
    width = d_gate.shape[1]
    deep = depth // 8
    return pl.pallas_call(
        paired_columns,
        grid=(depth // deep,),
        in_specs=[
            pl.BlockSpec((None, count, deep), lambda i: (0, 0, i)),
            pl.BlockSpec((count, width), lambda i: (0, 0)),
            pl.BlockSpec((count, width), lambda i: (0, 0)),
        ],
        out_specs=pl.BlockSpec((deep, 2, width), lambda i: (i, 0, 0)),
        out_shape=jax.ShapeDtypeStruct((depth, 2, width), jnp.bfloat16),
        cost_estimate=pl.CostEstimate(
            flops=4 * count * depth * width,
            bytes_accessed=4 * (depth * width + count * width + count * depth),
            transcendentals=0,
        ),
    )(packed, d_gate, d_up)


def swiglu_terms(gate, up, d_hidden):
    sig = jax.nn.sigmoid(gate)
    activated = gate * sig
    d_gate = d_hidden * up * (sig + gate * sig * (1.0 - sig))
    return activated * up, d_gate, d_hidden * activated


def block_terms(rows, cotangents, in_weight, down_weight):
    width = in_weight.shape[2]
    flat_in = in_weight.reshape(in_weight.shape[0], -1)
    d_hidden = exchange(dot(cotangents, down_weight, OVER_LAST), "row")
    projected = exchange(dot(rows, flat_in), "row")
    hidden, d_gate, d_up = swiglu_terms(projected[:, :width], projected[:, width:], d_hidden)
    d_local = jnp.concatenate([d_gate, d_up], 1).astype(jnp.bfloat16)
    hidden_all = gather(hidden.astype(jnp.bfloat16), "row")
    d_projected = gather(d_local, "row")
    mixed = exchange(dot(hidden_all, down_weight), "col").astype(jnp.bfloat16)
    d_down = dot(hidden_all, cotangents, OVER_FIRST).astype(jnp.bfloat16)
    d_tokens = exchange(dot(d_projected, flat_in, OVER_LAST), "col").astype(jnp.bfloat16)
    return (mixed, d_down, in_gradient(rows[None], d_projected[:, :width], d_projected[:, width:]), d_tokens)


def gather_kernel(
    size, side, tokens_ref, modality_ref, d_mixed_ref, packed_ref, pick_ref, count_ref,
    whole, chosen, local_sem, mate_send, mate_recv, send, recv, row_send, row_recv, hand_send, hand_recv,
):
    z, column = lax.axis_index("row"), lax.axis_index("col")
    core, chip = lax.rem(column, 2), column // 2
    y, x = chip // side, lax.rem(chip, side)
    rows = tokens_ref.shape[0]
    chips = side * side

    def at(part):
        return whole.at[pl.ds(pl.multiple_of(part * rows, rows), rows), :]

    def remote(src, dst, send_sem, recv_sem, where):
        return pltpu.make_async_remote_copy(
            src_ref=src, dst_ref=dst, send_sem=send_sem, recv_sem=recv_sem, device_id=where, device_id_type=MESH
        )

    def chip_of(dy, dx):
        return lax.rem(y + dy, side) * side + lax.rem(x + dx, side)

    mate = {"col": chip * 2 + 1 - core}
    others = [(dy, dx) for dy in range(side) for dx in range(side) if dy or dx]
    if side == 2:
        straight = [(0, 1), (1, 0)]
    else:
        straight = others

    def block_copy(k, source, half, dy, dx):
        part = source * 2 + half
        return remote(at(part), at(part), send.at[k], recv.at[part], {"col": chip_of(dy, dx) * 2 + core})

    def arrival(part):
        return remote(at(part), at(part), send.at[0], recv.at[part], mate)

    barrier = pltpu.get_barrier_semaphore()
    pl.semaphore_signal(barrier, inc=1, device_id=mate, device_id_type=MESH)
    for dy, dx in straight:
        pl.semaphore_signal(
            barrier, inc=1, device_id={"col": chip_of(dy, dx) * 2 + core}, device_id_type=MESH
        )
    for step in range(1, size):
        pl.semaphore_signal(barrier, inc=1, device_id={"row": lax.rem(z + step, size)}, device_id_type=MESH)
    mine = chip * 2 + core
    for k, (kept, given) in enumerate(((tokens_ref, d_mixed_ref), (d_mixed_ref, tokens_ref))):
        @pl.when(core == k)
        def _():
            pltpu.make_async_copy(kept, at(mine), local_sem.at[0]).start()

    pltpu.make_async_copy(modality_ref, chosen.at[z], local_sem.at[1]).start()
    pl.semaphore_wait(barrier, len(straight) + size)

    def mate_copy(given):
        return remote(given, at(mine), mate_send, mate_recv, mate)

    for k, given in enumerate((d_mixed_ref, tokens_ref)):
        @pl.when(core == k)
        def _():
            mate_copy(given).start()

    row_copies = [
        remote(
            modality_ref, chosen.at[z], row_send.at[step - 1], row_recv.at[step - 1],
            {"row": lax.rem(z + step, size)},
        )
        for step in range(1, size)
    ]
    for copy in row_copies:
        copy.start()
    pltpu.make_async_copy(tokens_ref, at(mine), local_sem.at[0]).wait()
    first = [block_copy(k, chip, core, dy, dx) for k, (dy, dx) in enumerate(straight)]
    for copy in first:
        copy.start()
    mate_copy(tokens_ref).wait_recv()
    base = len(straight)
    second = [block_copy(base + k, chip, 1 - core, dy, dx) for k, (dy, dx) in enumerate(straight)]
    for copy in second:
        copy.start()
    relays = []
    if side == 2:
        arrival(chip_of(0, 1) * 2).wait_recv()
        relays.append(block_copy(2 * base, chip_of(0, 1), 0, 1, 0))
        relays[-1].start()
        arrival(chip_of(1, 0) * 2 + 1).wait_recv()
        relays.append(block_copy(2 * base + 1, chip_of(1, 0), 1, 0, 1))
        relays[-1].start()

    pltpu.make_async_copy(modality_ref, chosen.at[z], local_sem.at[1]).wait()
    for copy in row_copies:
        copy.wait_recv()
    total = whole.shape[0]
    picked = jnp.concatenate([chosen[k] for k in range(size)], axis=1) == 1
    ones = jnp.broadcast_to(picked.astype(jnp.float32), (8, total))
    up_to = lax.broadcasted_iota(jnp.int32, (total, total), 0) <= lax.broadcasted_iota(
        jnp.int32, (total, total), 1
    )
    running = dot(ones.astype(jnp.bfloat16), up_to.astype(jnp.float32).astype(jnp.bfloat16))
    place = jnp.where(ones > 0.5, running, 0.0)[:1].astype(jnp.int32) - 1
    slot = lax.broadcasted_iota(jnp.int32, pick_ref.shape, 0)
    pick_ref[...] = (slot == place).astype(jnp.float32).astype(jnp.bfloat16)
    count_ref[...] = jnp.broadcast_to(jnp.sum(ones[:1], axis=1, keepdims=True), count_ref.shape)

    if side == 2:
        rest = [
            (chip_of(0, 1), 1), (chip_of(1, 0), 0), (chip_of(1, 1), 0), (chip_of(1, 1), 1),
        ]
    else:
        rest = [(chip_of(dy, dx), half) for dy, dx in others for half in range(2)]
    for source, half in rest:
        arrival(source * 2 + half).wait_recv()
    packed_ref[core] = dot(pick_ref[...], whole[...]).astype(jnp.bfloat16)
    hand = remote(packed_ref.at[core], packed_ref.at[core], hand_send, hand_recv, mate)
    hand.start()
    for copy in first + second + relays + row_copies:
        copy.wait_send()
    mate_copy(tokens_ref).wait_send()
    hand.wait_send()
    remote(packed_ref.at[1 - core], packed_ref.at[1 - core], hand_send, hand_recv, mate).wait_recv()


def gather_packed(tokens, modality, d_mixed, packed, collective_id):
    size, columns = lax.axis_size("row"), lax.axis_size("col")
    side = math.isqrt(columns // 2)
    rows, depth = tokens.shape
    total = rows * columns
    sends = 6 if side == 2 else 2 * (side * side - 1)
    vmem = pl.BlockSpec(memory_space=pltpu.VMEM)
    dma = pltpu.SemaphoreType.DMA
    return pl.pallas_call(
        functools.partial(gather_kernel, size, side),
        in_specs=[vmem] * 3,
        out_specs=[vmem] * 3,
        out_shape=[
            jax.ShapeDtypeStruct((2, packed, depth), jnp.bfloat16),
            jax.ShapeDtypeStruct((packed, total), jnp.bfloat16),
            jax.ShapeDtypeStruct((8, 128), jnp.float32),
        ],
        scratch_shapes=[
            pltpu.VMEM((total, depth), jnp.bfloat16),
            pltpu.VMEM((size, 1, total // size), jnp.int32),
            dma((2,)), dma, dma, dma((sends,)), dma((columns,)), dma((size - 1,)), dma((size - 1,)), dma, dma,
        ],
        compiler_params=pltpu.CompilerParams(collective_id=collective_id, has_side_effects=True),
        cost_estimate=pl.CostEstimate(
            flops=2 * packed * total * depth, bytes_accessed=4 * total * depth, transcendentals=0
        ),
    )(tokens, modality.reshape(1, -1), d_mixed)


def unpack(pairs_ref, columns_ref, apart):
    depth, _, wide = pairs_ref.shape
    tall = apart.shape[1] // 2
    for step in range(depth // tall):
        rows, buffer = slice(step * tall, (step + 1) * tall), step % apart.shape[0]
        apart[buffer] = pairs_ref[rows].reshape(2 * tall, wide).astype(jnp.float32)
        for part in range(2):
            one = apart[buffer, pl.ds(part, tall, stride=2), :]
            columns_ref[rows, part * wide:(part + 1) * wide] = one.astype(jnp.bfloat16)


def chain_kernel(
    size, units, wide, packed_ref, in_ref, down_ref, total_ref, hidden_ref, d_gate_ref, d_up_ref,
    raw, apart, w_down, w_in, partial, sums, terms,
    load_sem, sum_send, sum_recv, term_send, term_recv, out_sem,
):
    z = lax.axis_index("row")
    middle = size // 2
    slots = w_down.shape[0]
    held = partial.shape[0]
    near = jnp.minimum(z, size - 1 - z)
    last_lag = 2 * middle + 1 - near

    def owner_of(u):
        return middle - 1 + lax.rem(u, 2)

    def loads(u):
        columns = pl.ds(pl.multiple_of(u * wide, wide), wide)
        slot = lax.rem(u, 2)
        return (
            pltpu.make_async_copy(in_ref.at[:, :, columns], raw.at[slot], load_sem.at[0, slot]),
            pltpu.make_async_copy(down_ref.at[columns, :], w_down.at[lax.rem(u, slots)], load_sem.at[1, slot]),
        )

    def sum_copy(u, side):
        return pltpu.make_async_remote_copy(
            src_ref=sums.at[side, u], dst_ref=sums.at[side, u],
            send_sem=sum_send.at[u], recv_sem=sum_recv.at[side, u],
            device_id={"row": z + 1 - 2 * side}, device_id_type=MESH,
        )

    def term_copy(u, side):
        return pltpu.make_async_remote_copy(
            src_ref=terms.at[u], dst_ref=terms.at[u],
            send_sem=term_send.at[side, u], recv_sem=term_recv.at[u],
            device_id={"row": z + 1 - 2 * side}, device_id_type=MESH,
        )

    def out_copies(u):
        columns = pl.ds(pl.multiple_of(u * wide, wide), wide)
        return [
            pltpu.make_async_copy(
                terms.at[u, :, k * wide:(k + 1) * wide], ref.at[:, columns], out_sem.at[k, u]
            )
            for k, ref in enumerate((hidden_ref, d_gate_ref, d_up_ref))
        ]

    barrier = pltpu.get_barrier_semaphore()
    for step in (-1, 1):
        @pl.when((z + step >= 0) & (z + step < size))
        def _():
            pl.semaphore_signal(barrier, inc=1, device_id={"row": z + step}, device_id_type=MESH)
    for copy in loads(0):
        copy.start()
    total_ref[...] = jnp.zeros_like(total_ref)
    depth = down_ref.shape[1]
    pl.semaphore_wait(barrier, jnp.where(near > 0, 2, 1))

    @pl.loop(0, units + 2 * middle + 1)
    def _(t):
        @pl.when(t < units)
        def _():
            for copy in loads(t):
                copy.wait()

            @pl.when(t + 1 < units)
            def _():
                for copy in loads(t + 1):
                    copy.start()

            slot, here = lax.rem(t, slots), lax.rem(t, held)
            unpack(raw.at[lax.rem(t, 2)], w_in.at[slot], apart)
            partial[here, :, :2 * wide] = dot(packed_ref[0], w_in[slot])
            partial[here, :, 2 * wide:] = dot(packed_ref[1], w_down[slot], OVER_LAST)

        relayed = t - near

        @pl.when((relayed >= 0) & (relayed < units) & (owner_of(relayed) != z))
        def _():
            side = jnp.where(z < owner_of(relayed), 0, 1)
            here = lax.rem(relayed, held)

            @pl.when(near > 0)
            def _():
                sum_copy(relayed, side).wait_recv()
                sums[side, relayed] = (
                    partial[here] + sums[side, relayed].astype(jnp.float32)
                ).astype(sums.dtype)

            @pl.when(near == 0)
            def _():
                sums[side, relayed] = partial[here].astype(sums.dtype)

            sum_copy(relayed, side).start()

        closed = t - middle

        @pl.when((closed >= 0) & (closed < units) & (owner_of(closed) == z))
        def _():
            here = lax.rem(closed, held)

            @pl.when(z > 0)
            def _():
                sum_copy(closed, 0).wait_recv()
                partial[here] += sums[0, closed].astype(jnp.float32)

            @pl.when(z < size - 1)
            def _():
                sum_copy(closed, 1).wait_recv()
                partial[here] += sums[1, closed].astype(jnp.float32)

            whole = partial[here]
            results = swiglu_terms(*(whole[:, k * wide:(k + 1) * wide] for k in range(3)))
            for k, result in enumerate(results):
                terms[closed, :, k * wide:(k + 1) * wide] = result.astype(jnp.bfloat16)

            @pl.when(z < size - 1)
            def _():
                term_copy(closed, 0).start()

            @pl.when(z > 0)
            def _():
                term_copy(closed, 1).start()

        used = t - last_lag

        @pl.when((used >= 0) & (used < units))
        def _():
            owner = owner_of(used)

            @pl.when(owner != z)
            def _():
                side = jnp.where(z < owner, 1, 0)
                term_copy(used, side).wait_recv()

                @pl.when(near > 0)
                def _():
                    term_copy(used, side).start()

            for copy in out_copies(used):
                copy.start()
            slot = lax.rem(used, slots)
            total_ref[:, :depth] += dot(terms[used, :, :wide], w_down[slot])
            total_ref[:, depth:] += dot(terms[used, :, wide:], w_in[slot], OVER_LAST)

    @pl.loop(0, units)
    def _(u):
        owner = owner_of(u)
        for copy in out_copies(u):
            copy.wait()

        @pl.when(owner != z)
        def _():
            sum_copy(u, jnp.where(z < owner, 0, 1)).wait_send()

            @pl.when(near > 0)
            def _():
                term_copy(u, jnp.where(z < owner, 1, 0)).wait_send()

        @pl.when(owner == z)
        def _():
            @pl.when(z < size - 1)
            def _():
                term_copy(u, 0).wait_send()

            @pl.when(z > 0)
            def _():
                term_copy(u, 1).wait_send()


def chain(packed, in_weight, down_weight, collective_id):
    size = lax.axis_size("row")
    _, count, depth = packed.shape
    width = down_weight.shape[0]
    wide = 128
    units = width // wide
    slots = 2 * (size // 2) + 4
    held = size // 2 + 1
    sum_type = jnp.bfloat16 if size <= 4 else jnp.float32
    vmem, hbm = pl.BlockSpec(memory_space=pltpu.VMEM), pl.BlockSpec(memory_space=pl.ANY)
    dma = pltpu.SemaphoreType.DMA
    return pl.pallas_call(
        functools.partial(chain_kernel, size, units, wide),
        in_specs=[vmem, hbm, hbm],
        out_specs=[vmem, hbm, hbm, hbm],
        out_shape=[jax.ShapeDtypeStruct((count, 2 * depth), jnp.float32)]
        + 3 * [jax.ShapeDtypeStruct((count, width), jnp.bfloat16)],
        scratch_shapes=[
            pltpu.VMEM((2, depth, 2, wide), jnp.bfloat16),
            pltpu.VMEM((4, 128, wide), jnp.float32),
            pltpu.VMEM((slots, wide, depth), jnp.bfloat16),
            pltpu.VMEM((slots, depth, 2 * wide), jnp.bfloat16),
            pltpu.VMEM((held, count, 3 * wide), jnp.float32),
            pltpu.VMEM((2, units, count, 3 * wide), sum_type),
            pltpu.VMEM((units, count, 3 * wide), jnp.bfloat16),
            dma((2, 2)), dma((units,)), dma((2, units)), dma((2, units)), dma((units,)), dma((3, units)),
        ],
        compiler_params=pltpu.CompilerParams(
            collective_id=collective_id, has_side_effects=True, vmem_limit_bytes=60 * 1024 * 1024
        ),
        cost_estimate=pl.CostEstimate(
            flops=12 * count * depth * width, bytes_accessed=6 * depth * width, transcendentals=count * width
        ),
    )(packed, in_weight, down_weight)


def per_device(tokens, modality, in_weight, down_weight, d_mixed):
    total = tokens.shape[0] * lax.axis_size("col")
    depth = tokens.shape[1]
    room = total * 9 // 16
    packed, pick, count = gather_packed(tokens, modality, d_mixed, room, 2)

    def packed_form(packed, pick, tokens, modality, d_mixed, w_in, w_down):
        total, hidden, d_gate, d_up = chain(packed, w_in, w_down, 1)
        total = exchange(dot(pick, total.astype(jnp.bfloat16), OVER_FIRST), "col").astype(jnp.bfloat16)
        d_down = dot(hidden, packed[1], OVER_FIRST).astype(jnp.bfloat16)
        return (total[:, :depth], d_down, in_gradient(packed, d_gate, d_up), total[:, depth:])

    def whole_form(packed, pick, tokens, modality, d_mixed, w_in, w_down):
        keep = (gather(modality, "row") == 1)[:, None].astype(jnp.bfloat16)
        both = gather(jnp.concatenate([tokens, d_mixed], 1), "col") * keep
        return block_terms(both[:, :depth], both[:, depth:], w_in, w_down)

    return lax.cond(
        count[0, 0] <= room, packed_form, whole_form,
        packed, pick, tokens, modality, d_mixed, in_weight, down_weight,
    )


def solution(mesh):
    return jax.shard_map(
        per_device,
        mesh=mesh,
        in_specs=(
            P("col", "row"),
            P("row"),
            P("row", None, "col"),
            P("col", "row"),
            P("col", "row"),
        ),
        out_specs=(P("col", "row"), P("col", "row"), P("row", None, "col"), P("col", "row")),
        check_vma=False,
    )
```

```python
import functools
import math

import jax
import jax.numpy as jnp
from jax import lax
from jax.experimental import pallas as pl
from jax.experimental.pallas import tpu as pltpu
from jax.sharding import PartitionSpec as P

MESH = pl.DeviceIdType.MESH
OVER_LAST = (((1,), (1,)), ((), ()))
OVER_FIRST = (((0,), (0,)), ((), ()))


def dot(a, b, dims=(((1,), (0,)), ((), ()))):
    return lax.dot_general(a, b, dims, preferred_element_type=jnp.float32)


def gather(block, axis):
    count = lax.axis_size(axis)
    me = lax.axis_index(axis)
    out = jnp.zeros((count,) + block.shape, block.dtype)
    out = lax.dynamic_update_index_in_dim(out, block, me, 0)
    for shift in range(1, count):
        moves = [(i, (i + shift) % count) for i in range(count)]
        arrived = lax.ppermute(block, axis, moves)
        out = lax.dynamic_update_index_in_dim(out, arrived, lax.rem(me + count - shift, count), 0)
    return out.reshape((count * block.shape[0],) + block.shape[1:])


def chip_sum(blocks):
    columns = lax.axis_size("col")
    side = math.isqrt(columns // 2)
    total = blocks[0]
    for k in range(1, len(blocks)):
        dy, dx = divmod(k, side)
        moves = [
            (i, ((i // 2 // side + dy) % side * side + (i // 2 + dx) % side) * 2 + i % 2) for i in range(columns)
        ]
        total = total + lax.ppermute(blocks[k], "col", moves).astype(jnp.float32)
    return total


def paired_columns(tile, rows_ref, gate_ref, up_ref, out_ref):
    @pl.loop(0, gate_ref.shape[1] // tile)
    def _(step):
        columns = pl.ds(pl.multiple_of(step * tile, tile), tile)
        for part, side_ref in enumerate((gate_ref, up_ref)):
            out_ref[:, part, columns] = dot(rows_ref[...], side_ref[:, columns], OVER_FIRST).astype(jnp.bfloat16)


def in_gradient(packed, d_gate, d_up):
    depth = packed.shape[2]
    count, width = d_gate.shape
    deep = depth // 8
    tile = max(w for w in range(128, 1025, 128) if width % w == 0)
    return pl.pallas_call(
        functools.partial(paired_columns, tile),
        grid=(depth // deep,),
        in_specs=[
            pl.BlockSpec((None, count, deep), lambda i: (0, 0, i)),
            pl.BlockSpec((count, width), lambda i: (0, 0)),
            pl.BlockSpec((count, width), lambda i: (0, 0)),
        ],
        out_specs=pl.BlockSpec((deep, 2, width), lambda i: (i, 0, 0)),
        out_shape=jax.ShapeDtypeStruct((depth, 2, width), jnp.bfloat16),
        cost_estimate=pl.CostEstimate(
            flops=4 * count * depth * width,
            bytes_accessed=4 * (depth * width + count * width + count * depth),
            transcendentals=0,
        ),
    )(packed, d_gate, d_up)


def swiglu_terms(gate, up, d_hidden):
    sig = jax.nn.sigmoid(gate)
    activated = gate * sig
    d_gate = d_hidden * up * (sig + gate * sig * (1.0 - sig))
    return activated * up, d_gate, d_hidden * activated


def gather_kernel(
    size, side, tokens_ref, modality_ref, d_mixed_ref, packed_ref, pick_ref, count_ref,
    whole, chosen, local_sem, mate_send, mate_recv, send, recv, row_send, row_recv, hand_send, hand_recv,
):
    z, column = lax.axis_index("row"), lax.axis_index("col")
    core, chip = lax.rem(column, 2), column // 2
    y, x = chip // side, lax.rem(chip, side)
    rows = tokens_ref.shape[0]
    chips = side * side

    def at(part):
        return whole.at[pl.ds(pl.multiple_of(part * rows, rows), rows), :]

    def remote(src, dst, send_sem, recv_sem, where):
        return pltpu.make_async_remote_copy(
            src_ref=src, dst_ref=dst, send_sem=send_sem, recv_sem=recv_sem, device_id=where, device_id_type=MESH
        )

    def chip_of(dy, dx):
        return lax.rem(y + dy, side) * side + lax.rem(x + dx, side)

    mate = {"col": chip * 2 + 1 - core}
    others = [(dy, dx) for dy in range(side) for dx in range(side) if dy or dx]
    if side == 2:
        straight = [(0, 1), (1, 0)]
    else:
        straight = others

    def block_copy(k, source, half, dy, dx):
        part = source * 2 + half
        return remote(at(part), at(part), send.at[k], recv.at[part], {"col": chip_of(dy, dx) * 2 + core})

    def arrival(part):
        return remote(at(part), at(part), send.at[0], recv.at[part], mate)

    barrier = pltpu.get_barrier_semaphore()
    pl.semaphore_signal(barrier, inc=1, device_id=mate, device_id_type=MESH)
    for dy, dx in straight:
        pl.semaphore_signal(
            barrier, inc=1, device_id={"col": chip_of(dy, dx) * 2 + core}, device_id_type=MESH
        )
    for step in range(1, size):
        pl.semaphore_signal(barrier, inc=1, device_id={"row": lax.rem(z + step, size)}, device_id_type=MESH)
    mine = chip * 2 + core
    for k, (kept, given) in enumerate(((tokens_ref, d_mixed_ref), (d_mixed_ref, tokens_ref))):
        @pl.when(core == k)
        def _():
            pltpu.make_async_copy(kept, at(mine), local_sem.at[0]).start()

    pltpu.make_async_copy(modality_ref, chosen.at[z], local_sem.at[1]).start()
    pl.semaphore_wait(barrier, len(straight) + size)

    def mate_copy(given):
        return remote(given, at(mine), mate_send, mate_recv, mate)

    for k, given in enumerate((d_mixed_ref, tokens_ref)):
        @pl.when(core == k)
        def _():
            mate_copy(given).start()

    row_copies = [
        remote(
            modality_ref, chosen.at[z], row_send.at[step - 1], row_recv.at[step - 1],
            {"row": lax.rem(z + step, size)},
        )
        for step in range(1, size)
    ]
    for copy in row_copies:
        copy.start()
    pltpu.make_async_copy(tokens_ref, at(mine), local_sem.at[0]).wait()
    first = [block_copy(k, chip, core, dy, dx) for k, (dy, dx) in enumerate(straight)]
    for copy in first:
        copy.start()
    mate_copy(tokens_ref).wait_recv()
    base = len(straight)
    second = [block_copy(base + k, chip, 1 - core, dy, dx) for k, (dy, dx) in enumerate(straight)]
    for copy in second:
        copy.start()
    relays = []
    if side == 2:
        arrival(chip_of(0, 1) * 2).wait_recv()
        relays.append(block_copy(2 * base, chip_of(0, 1), 0, 1, 0))
        relays[-1].start()
        arrival(chip_of(1, 0) * 2 + 1).wait_recv()
        relays.append(block_copy(2 * base + 1, chip_of(1, 0), 1, 0, 1))
        relays[-1].start()

    pltpu.make_async_copy(modality_ref, chosen.at[z], local_sem.at[1]).wait()
    for copy in row_copies:
        copy.wait_recv()
    total = whole.shape[0]
    picked = jnp.concatenate([chosen[k] for k in range(size)], axis=1) == 1
    ones = jnp.broadcast_to(picked.astype(jnp.float32), (8, total))
    up_to = lax.broadcasted_iota(jnp.int32, (total, total), 0) <= lax.broadcasted_iota(
        jnp.int32, (total, total), 1
    )
    running = dot(ones.astype(jnp.bfloat16), up_to.astype(jnp.float32).astype(jnp.bfloat16))
    place = jnp.where(ones > 0.5, running, 0.0)[:1].astype(jnp.int32) - 1
    slot = lax.broadcasted_iota(jnp.int32, pick_ref.shape, 0)
    pick_ref[...] = (slot == place).astype(jnp.float32).astype(jnp.bfloat16)
    count_ref[...] = jnp.broadcast_to(jnp.sum(ones[:1], axis=1, keepdims=True), count_ref.shape)

    if side == 2:
        rest = [
            (chip_of(0, 1), 1), (chip_of(1, 0), 0), (chip_of(1, 1), 0), (chip_of(1, 1), 1),
        ]
    else:
        rest = [(chip_of(dy, dx), half) for dy, dx in others for half in range(2)]
    for source, half in rest:
        arrival(source * 2 + half).wait_recv()
    packed_ref[core] = dot(pick_ref[...], whole[...]).astype(jnp.bfloat16)
    hand = remote(packed_ref.at[core], packed_ref.at[core], hand_send, hand_recv, mate)
    hand.start()
    for copy in first + second + relays + row_copies:
        copy.wait_send()
    mate_copy(tokens_ref).wait_send()
    hand.wait_send()
    remote(packed_ref.at[1 - core], packed_ref.at[1 - core], hand_send, hand_recv, mate).wait_recv()


def gather_packed(tokens, modality, d_mixed, packed, collective_id):
    size, columns = lax.axis_size("row"), lax.axis_size("col")
    side = math.isqrt(columns // 2)
    rows, depth = tokens.shape
    total = rows * columns
    sends = 6 if side == 2 else 2 * (side * side - 1)
    vmem = pl.BlockSpec(memory_space=pltpu.VMEM)
    dma = pltpu.SemaphoreType.DMA
    return pl.pallas_call(
        functools.partial(gather_kernel, size, side),
        in_specs=[vmem] * 3,
        out_specs=[vmem] * 3,
        out_shape=[
            jax.ShapeDtypeStruct((2, packed, depth), jnp.bfloat16),
            jax.ShapeDtypeStruct((packed, total), jnp.bfloat16),
            jax.ShapeDtypeStruct((8, 128), jnp.float32),
        ],
        scratch_shapes=[
            pltpu.VMEM((total, depth), jnp.bfloat16),
            pltpu.VMEM((size, 1, total // size), jnp.int32),
            dma((2,)), dma, dma, dma((sends,)), dma((columns,)), dma((size - 1,)), dma((size - 1,)), dma, dma,
        ],
        compiler_params=pltpu.CompilerParams(collective_id=collective_id, has_side_effects=True),
        cost_estimate=pl.CostEstimate(
            flops=2 * packed * total * depth, bytes_accessed=4 * total * depth, transcendentals=0
        ),
    )(tokens, modality.reshape(1, -1), d_mixed)


def unpack(pairs_ref, columns_ref, apart):
    depth, _, wide = pairs_ref.shape
    tall = apart.shape[1] // 2
    buffers = apart.shape[0]

    @pl.loop(0, depth // (tall * buffers))
    def _(step):
        for buffer in range(buffers):
            rows = pl.ds(pl.multiple_of((step * buffers + buffer) * tall, tall), tall)
            apart[buffer] = pairs_ref[rows].reshape(2 * tall, wide).astype(jnp.float32)
            for part in range(2):
                one = apart[buffer, pl.ds(part, tall, stride=2), :]
                columns_ref[rows, part * wide:(part + 1) * wide] = one.astype(jnp.bfloat16)


def chain_kernel(
    size, side, units, wide, packed_ref, pick_ref, in_ref, down_ref, hidden_ref, d_gate_ref, d_up_ref, own_ref, *rest
):
    other_refs, scratch = rest[:side * side - 1], rest[side * side - 1:]
    (
        total_ref, pick_rows, mine, given, got, raw, apart, w_down, w_in, partial, sums, terms,
        load_sem, sum_send, sum_recv, term_send, term_recv, out_sem, pair_send, pair_recv,
    ) = scratch
    z, column = lax.axis_index("row"), lax.axis_index("col")
    core, chip = lax.rem(column, 2), column // 2
    mate = {"col": chip * 2 + 1 - core}
    shifts = [(dy, dx) for dy in range(side) for dx in range(side)]
    middle = size // 2
    slots = w_down.shape[0]
    held = partial.shape[0]
    near = jnp.minimum(z, size - 1 - z)
    count = partial.shape[1]
    cut = count // 16 * 8
    spans = (slice(0, cut), slice(cut, count))

    def owner_of(u):
        return middle - 1 + lax.rem(u, 2)

    def loads(u):
        columns = pl.ds(pl.multiple_of(u * wide, wide), wide)
        slot = lax.rem(u, 2)
        return (
            pltpu.make_async_copy(in_ref.at[:, :, columns], raw.at[slot], load_sem.at[0, slot]),
            pltpu.make_async_copy(down_ref.at[columns, :], w_down.at[lax.rem(u, slots)], load_sem.at[1, slot]),
        )

    def sum_copy(u, side, h):
        return pltpu.make_async_remote_copy(
            src_ref=sums.at[side, u, spans[h]], dst_ref=sums.at[side, u, spans[h]],
            send_sem=sum_send.at[h, u], recv_sem=sum_recv.at[h, side, u],
            device_id={"row": z + 1 - 2 * side}, device_id_type=MESH,
        )

    def term_copy(u, side, h):
        return pltpu.make_async_remote_copy(
            src_ref=terms.at[u, spans[h]], dst_ref=terms.at[u, spans[h]],
            send_sem=term_send.at[h, side, u], recv_sem=term_recv.at[h, u],
            device_id={"row": z + 1 - 2 * side}, device_id_type=MESH,
        )

    def out_copies(u):
        columns = pl.ds(pl.multiple_of(u * wide, wide), wide)
        return [
            pltpu.make_async_copy(
                terms.at[u, :, k * wide:(k + 1) * wide], ref.at[:, columns], out_sem.at[k, u]
            )
            for k, ref in enumerate((hidden_ref, d_gate_ref, d_up_ref))
        ]

    barrier = pltpu.get_barrier_semaphore()
    for step in (-1, 1):
        @pl.when((z + step >= 0) & (z + step < size))
        def _():
            pl.semaphore_signal(barrier, inc=1, device_id={"row": z + step}, device_id_type=MESH)
    pl.semaphore_signal(barrier, inc=1, device_id=mate, device_id_type=MESH)
    for copy in loads(0):
        copy.start()
    @pl.loop(0, count // 8)
    def _(step):
        total_ref[pl.ds(pl.multiple_of(step * 8, 8), 8), :] = jnp.zeros((8, total_ref.shape[1]), jnp.float32)

    depth = down_ref.shape[1]
    rows = own_ref.shape[0]
    same = lax.broadcasted_iota(jnp.int32, (count, count), 0) == lax.broadcasted_iota(jnp.int32, (count, count), 1)
    turned = dot(pick_ref[:count], same.astype(jnp.float32).astype(jnp.bfloat16), OVER_FIRST)
    pick_rows[...] = turned.astype(jnp.bfloat16)
    pl.semaphore_wait(barrier, jnp.where(near > 0, 3, 2))

    @pl.loop(0, units + 2 * middle + 3)
    def _(t):
        @pl.when(t < units)
        def _():
            for copy in loads(t):
                copy.wait()

            @pl.when(t + 1 < units)
            def _():
                for copy in loads(t + 1):
                    copy.start()

            slot, here = lax.rem(t, slots), lax.rem(t, held)
            unpack(raw.at[lax.rem(t, 2)], w_in.at[slot], apart)
            partial[here, :, :2 * wide] = dot(packed_ref[0, :count], w_in[slot])
            partial[here, :, 2 * wide:] = dot(packed_ref[1, :count], w_down[slot], OVER_LAST)

        relayed = t - near

        @pl.when((relayed >= 0) & (relayed < units) & (owner_of(relayed) != z))
        def _():
            side = jnp.where(z < owner_of(relayed), 0, 1)
            here = lax.rem(relayed, held)
            for h, span in enumerate(spans):
                @pl.when(near > 0)
                def _():
                    sum_copy(relayed, side, h).wait_recv()
                    sums[side, relayed, span] = (
                        partial[here, span] + sums[side, relayed, span].astype(jnp.float32)
                    ).astype(sums.dtype)

                @pl.when(near == 0)
                def _():
                    sums[side, relayed, span] = partial[here, span].astype(sums.dtype)

                sum_copy(relayed, side, h).start()

        closed = t - middle

        @pl.when((closed >= 0) & (closed < units) & (owner_of(closed) == z))
        def _():
            here = lax.rem(closed, held)
            for h, span in enumerate(spans):
                @pl.when(z > 0)
                def _():
                    sum_copy(closed, 0, h).wait_recv()
                    partial[here, span] += sums[0, closed, span].astype(jnp.float32)

                @pl.when(z < size - 1)
                def _():
                    sum_copy(closed, 1, h).wait_recv()
                    partial[here, span] += sums[1, closed, span].astype(jnp.float32)

                results = swiglu_terms(*(partial[here, span, k * wide:(k + 1) * wide] for k in range(3)))
                for k, result in enumerate(results):
                    terms[closed, span, k * wide:(k + 1) * wide] = result.astype(jnp.bfloat16)

                @pl.when(z < size - 1)
                def _():
                    term_copy(closed, 0, h).start()

                @pl.when(z > 0)
                def _():
                    term_copy(closed, 1, h).start()

        passed = t - (2 * middle + 2 - near)

        @pl.when((passed >= 0) & (passed < units) & (owner_of(passed) != z) & (near > 0))
        def _():
            side = jnp.where(z < owner_of(passed), 1, 0)
            for h in range(2):
                term_copy(passed, side, h).wait_recv()
                term_copy(passed, side, h).start()

        used = t - (2 * middle + 3 - near)

        @pl.when((used >= 0) & (used < units))
        def _():
            @pl.when((owner_of(used) != z) & (near == 0))
            def _():
                for h in range(2):
                    term_copy(used, 0, h).wait_recv()

            for copy in out_copies(used):
                copy.start()
            slot = lax.rem(used, slots)
            total_ref[:, :depth] += dot(terms[used, :, :wide], w_down[slot])
            total_ref[:, depth:] += dot(terms[used, :, wide:], w_in[slot], OVER_LAST)

    span = mine.shape[2]

    def pair_copy(b):
        return pltpu.make_async_remote_copy(
            src_ref=given.at[b], dst_ref=got.at[b], send_sem=pair_send.at[b], recv_sem=pair_recv.at[b],
            device_id=mate, device_id_type=MESH,
        )

    def chosen_rows(which):
        parts = []
        for dy, dx in shifts:
            there = lax.rem(chip // side + dy, side) * side + lax.rem(lax.rem(chip, side) + dx, side)
            start = pl.multiple_of((there * 2 + which) * rows, rows)
            parts.append(pick_rows[pl.ds(start, rows), :])
        return jnp.concatenate(parts, axis=0)

    ours, theirs = chosen_rows(core), chosen_rows(1 - core)

    @pl.loop(0, mine.shape[0])
    def _(b):
        part = total_ref[:, pl.ds(pl.multiple_of(b * span, span), span)]
        high = part.astype(jnp.bfloat16)
        low = (part - high.astype(jnp.float32)).astype(jnp.bfloat16)
        given[b] = (dot(theirs, high) + dot(theirs, low)).astype(jnp.bfloat16)
        pair_copy(b).start()
        mine[b] = dot(ours, high) + dot(ours, low)

    @pl.loop(0, mine.shape[0])
    def _(b):
        pair_copy(b).wait_recv()
        columns = pl.ds(pl.multiple_of(b * span, span), span)
        both = mine[b] + got[b].astype(jnp.float32)
        for k, ref in enumerate((own_ref,) + tuple(other_refs)):
            ref[:, columns] = both[k * rows:(k + 1) * rows].astype(ref.dtype)

    @pl.loop(0, mine.shape[0])
    def _(b):
        pair_copy(b).wait_send()

    @pl.loop(0, units)
    def _(u):
        owner = owner_of(u)
        for copy in out_copies(u):
            copy.wait()

        @pl.when(owner != z)
        def _():
            for h in range(2):
                sum_copy(u, jnp.where(z < owner, 0, 1), h).wait_send()

            @pl.when(near > 0)
            def _():
                for h in range(2):
                    term_copy(u, jnp.where(z < owner, 1, 0), h).wait_send()

        @pl.when(owner == z)
        def _():
            @pl.when(z < size - 1)
            def _():
                for h in range(2):
                    term_copy(u, 0, h).wait_send()

            @pl.when(z > 0)
            def _():
                for h in range(2):
                    term_copy(u, 1, h).wait_send()


def chain(packed, pick, count, in_weight, down_weight, collective_id):
    size, columns = lax.axis_size("row"), lax.axis_size("col")
    side = math.isqrt(columns // 2)
    chips, rows = side * side, pick.shape[1] // columns
    blocks = 8
    depth = packed.shape[2]
    width = down_weight.shape[0]
    wide = 128
    units = width // wide
    slots = 2 * (size // 2) + 6
    held = size // 2 + 1
    sum_type = jnp.bfloat16 if size <= 4 else jnp.float32
    vmem, hbm = pl.BlockSpec(memory_space=pltpu.VMEM), pl.BlockSpec(memory_space=pl.ANY)
    dma = pltpu.SemaphoreType.DMA
    return pl.pallas_call(
        functools.partial(chain_kernel, size, side, units, wide),
        in_specs=[vmem, vmem, hbm, hbm],
        out_specs=[hbm] * 3 + [vmem] * chips,
        out_shape=[jax.ShapeDtypeStruct((count, width), jnp.bfloat16)] * 3
        + [jax.ShapeDtypeStruct((rows, 2 * depth), jnp.float32)]
        + [jax.ShapeDtypeStruct((rows, 2 * depth), jnp.bfloat16)] * (chips - 1),
        scratch_shapes=[
            pltpu.VMEM((count, 2 * depth), jnp.float32),
            pltpu.VMEM((pick.shape[1], count), jnp.bfloat16),
            pltpu.VMEM((blocks, chips * rows, 2 * depth // blocks), jnp.float32),
            pltpu.VMEM((blocks, chips * rows, 2 * depth // blocks), jnp.bfloat16),
            pltpu.VMEM((blocks, chips * rows, 2 * depth // blocks), jnp.bfloat16),
            pltpu.VMEM((2, depth, 2, wide), jnp.bfloat16),
            pltpu.VMEM((8, 128, wide), jnp.float32),
            pltpu.VMEM((slots, wide, depth), jnp.bfloat16),
            pltpu.VMEM((slots, depth, 2 * wide), jnp.bfloat16),
            pltpu.VMEM((held, count, 3 * wide), jnp.float32),
            pltpu.VMEM((2, units, count, 3 * wide), sum_type),
            pltpu.VMEM((units, count, 3 * wide), jnp.bfloat16),
            dma((2, 2)), dma((2, units)), dma((2, 2, units)), dma((2, 2, units)), dma((2, units)), dma((3, units)),
            dma((blocks,)), dma((blocks,)),
        ],
        compiler_params=pltpu.CompilerParams(
            collective_id=collective_id, has_side_effects=True, vmem_limit_bytes=60 * 1024 * 1024
        ),
        cost_estimate=pl.CostEstimate(
            flops=12 * count * depth * width, bytes_accessed=6 * depth * width, transcendentals=count * width
        ),
    )(packed, pick, in_weight, down_weight)


def per_device(tokens, modality, in_weight, down_weight, d_mixed):
    total = tokens.shape[0] * lax.axis_size("col")
    depth = tokens.shape[1]
    rooms = (total // 2, total * 9 // 16)
    packed, pick, count = gather_packed(tokens, modality, d_mixed, rooms[-1], 1)

    def gradients(packed, hidden, d_gate, d_up, blocks):
        mine = chip_sum(blocks).astype(jnp.bfloat16)
        d_down = dot(hidden, packed[1, :hidden.shape[0]], OVER_FIRST).astype(jnp.bfloat16)
        return (mine[:, :depth], d_down, in_gradient(packed, d_gate, d_up), mine[:, depth:])

    def packed_form(room, collective_id, packed, pick, tokens, modality, d_mixed, w_in, w_down):
        hidden, d_gate, d_up, *blocks = chain(packed, pick, room, w_in, w_down, collective_id)
        return gradients(packed, hidden, d_gate, d_up, blocks)

    def whole_form(packed, pick, tokens, modality, d_mixed, w_in, w_down):
        keep = (gather(modality, "row") == 1)[:, None].astype(jnp.bfloat16)
        both = gather(jnp.concatenate([tokens, d_mixed], 1), "col") * keep
        both = both.reshape(total, 2, depth).transpose(1, 0, 2)
        room = total // 2

        def half_of(k):
            part = lax.dynamic_slice_in_dim(both, k * room, room, 1)
            spots = jnp.arange(room)[:, None] + k * room == jnp.arange(total)[None, :]
            return chain(part, spots.astype(jnp.bfloat16), room, w_in, w_down, 2 + len(rooms))

        outs = lax.map(lambda k: lax.optimization_barrier(half_of(k)), jnp.arange(2))
        hidden, d_gate, d_up = (x.reshape(total, -1) for x in outs[:3])
        return gradients(both, hidden, d_gate, d_up, [x[0] + x[1] for x in outs[3:]])

    forms = [functools.partial(packed_form, room, 2 + k) for k, room in enumerate(rooms)] + [whole_form]
    chosen = sum((count[0, 0] > room).astype(jnp.int32) for room in rooms)
    return lax.switch(chosen, forms, packed, pick, tokens, modality, d_mixed, in_weight, down_weight)


def solution(mesh):
    return jax.shard_map(
        per_device,
        mesh=mesh,
        in_specs=(
            P("col", "row"),
            P("row"),
            P("row", None, "col"),
            P("col", "row"),
            P("col", "row"),
        ),
        out_specs=(P("col", "row"), P("col", "row"), P("row", None, "col"), P("col", "row")),
        check_vma=False,
    )
```

```python
import functools
import math

import jax
import jax.numpy as jnp
from jax import lax
from jax.experimental import pallas as pl
from jax.experimental.pallas import tpu as pltpu
from jax.sharding import PartitionSpec as P

MESH = pl.DeviceIdType.MESH
OVER_LAST = (((1,), (1,)), ((), ()))
OVER_FIRST = (((0,), (0,)), ((), ()))


def dot(a, b, dims=(((1,), (0,)), ((), ()))):
    return lax.dot_general(a, b, dims, preferred_element_type=jnp.float32)


def gather(block, axis):
    count = lax.axis_size(axis)
    me = lax.axis_index(axis)
    out = jnp.zeros((count,) + block.shape, block.dtype)
    out = lax.dynamic_update_index_in_dim(out, block, me, 0)
    for shift in range(1, count):
        moves = [(i, (i + shift) % count) for i in range(count)]
        arrived = lax.ppermute(block, axis, moves)
        out = lax.dynamic_update_index_in_dim(out, arrived, lax.rem(me + count - shift, count), 0)
    return out.reshape((count * block.shape[0],) + block.shape[1:])


def chip_sum(blocks):
    columns = lax.axis_size("col")
    side = math.isqrt(columns // 2)
    total = blocks[0]
    for k in range(1, len(blocks)):
        dy, dx = divmod(k, side)
        moves = [
            (i, ((i // 2 // side + dy) % side * side + (i // 2 + dx) % side) * 2 + i % 2) for i in range(columns)
        ]
        total = total + lax.ppermute(blocks[k], "col", moves).astype(jnp.float32)
    return total


def paired_columns(tile, rows_ref, gate_ref, up_ref, out_ref):
    def some(columns):
        for part, side_ref in enumerate((gate_ref, up_ref)):
            out_ref[:, part, columns] = dot(rows_ref[...], side_ref[:, columns], OVER_FIRST).astype(jnp.bfloat16)

    if tile == gate_ref.shape[1]:
        some(slice(None))
    else:
        pl.loop(0, gate_ref.shape[1] // tile)(
            lambda step: some(pl.ds(pl.multiple_of(step * tile, tile), tile))
        )


def in_gradient(packed, d_gate, d_up, widest):
    depth = packed.shape[2]
    count, width = d_gate.shape
    deep = depth // 8
    tile = max(w for w in range(128, min(width, widest) + 1, 128) if width % w == 0)
    return pl.pallas_call(
        functools.partial(paired_columns, tile),
        grid=(depth // deep,),
        in_specs=[
            pl.BlockSpec((None, count, deep), lambda i: (0, 0, i)),
            pl.BlockSpec((count, width), lambda i: (0, 0)),
            pl.BlockSpec((count, width), lambda i: (0, 0)),
        ],
        out_specs=pl.BlockSpec((deep, 2, width), lambda i: (i, 0, 0)),
        out_shape=jax.ShapeDtypeStruct((depth, 2, width), jnp.bfloat16),
        cost_estimate=pl.CostEstimate(
            flops=4 * count * depth * width,
            bytes_accessed=4 * (depth * width + count * width + count * depth),
            transcendentals=0,
        ),
    )(packed, d_gate, d_up)


def swiglu_terms(gate, up, d_hidden):
    sig = jax.nn.sigmoid(gate)
    activated = gate * sig
    d_gate = d_hidden * up * (sig + gate * sig * (1.0 - sig))
    return activated * up, d_gate, d_hidden * activated


def gather_kernel(
    size, side, tokens_ref, modality_ref, d_mixed_ref, packed_ref, pick_ref, count_ref,
    whole, chosen, local_sem, mate_send, mate_recv, send, recv, row_send, row_recv, hand_send, hand_recv,
):
    z, column = lax.axis_index("row"), lax.axis_index("col")
    core, chip = lax.rem(column, 2), column // 2
    y, x = chip // side, lax.rem(chip, side)
    rows = tokens_ref.shape[0]
    chips = side * side

    def at(part):
        return whole.at[pl.ds(pl.multiple_of(part * rows, rows), rows), :]

    def remote(src, dst, send_sem, recv_sem, where):
        return pltpu.make_async_remote_copy(
            src_ref=src, dst_ref=dst, send_sem=send_sem, recv_sem=recv_sem, device_id=where, device_id_type=MESH
        )

    def chip_of(dy, dx):
        return lax.rem(y + dy, side) * side + lax.rem(x + dx, side)

    mate = {"col": chip * 2 + 1 - core}
    others = [(dy, dx) for dy in range(side) for dx in range(side) if dy or dx]
    if side == 2:
        straight = [(0, 1), (1, 0)]
    else:
        straight = others

    def block_copy(k, source, half, dy, dx):
        part = source * 2 + half
        return remote(at(part), at(part), send.at[k], recv.at[part], {"col": chip_of(dy, dx) * 2 + core})

    def arrival(part):
        return remote(at(part), at(part), send.at[0], recv.at[part], mate)

    barrier = pltpu.get_barrier_semaphore()
    pl.semaphore_signal(barrier, inc=1, device_id=mate, device_id_type=MESH)
    for dy, dx in straight:
        pl.semaphore_signal(
            barrier, inc=1, device_id={"col": chip_of(dy, dx) * 2 + core}, device_id_type=MESH
        )
    for step in range(1, size):
        pl.semaphore_signal(barrier, inc=1, device_id={"row": lax.rem(z + step, size)}, device_id_type=MESH)
    mine = chip * 2 + core
    for k, (kept, given) in enumerate(((tokens_ref, d_mixed_ref), (d_mixed_ref, tokens_ref))):
        @pl.when(core == k)
        def _():
            pltpu.make_async_copy(kept, at(mine), local_sem.at[0]).start()

    pltpu.make_async_copy(modality_ref, chosen.at[z], local_sem.at[1]).start()
    pl.semaphore_wait(barrier, len(straight) + size)

    def mate_copy(given):
        return remote(given, at(mine), mate_send, mate_recv, mate)

    for k, given in enumerate((d_mixed_ref, tokens_ref)):
        @pl.when(core == k)
        def _():
            mate_copy(given).start()

    row_copies = [
        remote(
            modality_ref, chosen.at[z], row_send.at[step - 1], row_recv.at[step - 1],
            {"row": lax.rem(z + step, size)},
        )
        for step in range(1, size)
    ]
    for copy in row_copies:
        copy.start()
    pltpu.make_async_copy(tokens_ref, at(mine), local_sem.at[0]).wait()
    first = [block_copy(k, chip, core, dy, dx) for k, (dy, dx) in enumerate(straight)]
    for copy in first:
        copy.start()
    mate_copy(tokens_ref).wait_recv()
    base = len(straight)
    second = [block_copy(base + k, chip, 1 - core, dy, dx) for k, (dy, dx) in enumerate(straight)]
    for copy in second:
        copy.start()
    relays = []
    if side == 2:
        arrival(chip_of(0, 1) * 2).wait_recv()
        relays.append(block_copy(2 * base, chip_of(0, 1), 0, 1, 0))
        relays[-1].start()
        arrival(chip_of(1, 0) * 2 + 1).wait_recv()
        relays.append(block_copy(2 * base + 1, chip_of(1, 0), 1, 0, 1))
        relays[-1].start()

    pltpu.make_async_copy(modality_ref, chosen.at[z], local_sem.at[1]).wait()
    for copy in row_copies:
        copy.wait_recv()
    total = whole.shape[0]
    picked = jnp.concatenate([chosen[k] for k in range(size)], axis=1) == 1
    ones = jnp.broadcast_to(picked.astype(jnp.float32), (8, total))
    up_to = lax.broadcasted_iota(jnp.int32, (total, total), 0) <= lax.broadcasted_iota(
        jnp.int32, (total, total), 1
    )
    running = dot(ones.astype(jnp.bfloat16), up_to.astype(jnp.float32).astype(jnp.bfloat16))
    place = jnp.where(ones > 0.5, running, 0.0)[:1].astype(jnp.int32) - 1
    slot = lax.broadcasted_iota(jnp.int32, pick_ref.shape, 0)
    pick_ref[...] = (slot == place).astype(jnp.float32).astype(jnp.bfloat16)
    count_ref[...] = jnp.broadcast_to(jnp.sum(ones[:1], axis=1, keepdims=True), count_ref.shape)

    if side == 2:
        rest = [
            (chip_of(0, 1), 1), (chip_of(1, 0), 0), (chip_of(1, 1), 0), (chip_of(1, 1), 1),
        ]
    else:
        rest = [(chip_of(dy, dx), half) for dy, dx in others for half in range(2)]
    for source, half in rest:
        arrival(source * 2 + half).wait_recv()
    packed_ref[core] = dot(pick_ref[...], whole[...]).astype(jnp.bfloat16)
    hand = remote(packed_ref.at[core], packed_ref.at[core], hand_send, hand_recv, mate)
    hand.start()
    for copy in first + second + relays + row_copies:
        copy.wait_send()
    mate_copy(tokens_ref).wait_send()
    hand.wait_send()
    remote(packed_ref.at[1 - core], packed_ref.at[1 - core], hand_send, hand_recv, mate).wait_recv()


def gather_packed(tokens, modality, d_mixed, packed, collective_id):
    size, columns = lax.axis_size("row"), lax.axis_size("col")
    side = math.isqrt(columns // 2)
    rows, depth = tokens.shape
    total = rows * columns
    sends = 6 if side == 2 else 2 * (side * side - 1)
    vmem = pl.BlockSpec(memory_space=pltpu.VMEM)
    dma = pltpu.SemaphoreType.DMA
    return pl.pallas_call(
        functools.partial(gather_kernel, size, side),
        in_specs=[vmem] * 3,
        out_specs=[vmem] * 3,
        out_shape=[
            jax.ShapeDtypeStruct((2, packed, depth), jnp.bfloat16),
            jax.ShapeDtypeStruct((packed, total), jnp.bfloat16),
            jax.ShapeDtypeStruct((8, 128), jnp.float32),
        ],
        scratch_shapes=[
            pltpu.VMEM((total, depth), jnp.bfloat16),
            pltpu.VMEM((size, 1, total // size), jnp.int32),
            dma((2,)), dma, dma, dma((sends,)), dma((columns,)), dma((size - 1,)), dma((size - 1,)), dma, dma,
        ],
        compiler_params=pltpu.CompilerParams(collective_id=collective_id, has_side_effects=True),
        cost_estimate=pl.CostEstimate(
            flops=2 * packed * total * depth, bytes_accessed=4 * total * depth, transcendentals=0
        ),
    )(tokens, modality.reshape(1, -1), d_mixed)


def unpack(pairs_ref, columns_ref, apart):
    depth, _, wide = pairs_ref.shape
    tall = apart.shape[1] // 2
    for step in range(depth // tall):
        rows, buffer = slice(step * tall, (step + 1) * tall), step % apart.shape[0]
        apart[buffer] = pairs_ref[rows].reshape(2 * tall, wide).astype(jnp.float32)
        for part in range(2):
            one = apart[buffer, pl.ds(part, tall, stride=2), :]
            columns_ref[rows, part * wide:(part + 1) * wide] = one.astype(jnp.bfloat16)


def chain_kernel(
    size, side, units, wide, packed_ref, pick_ref, in_ref, down_ref, hidden_ref, d_gate_ref, d_up_ref, own_ref, *rest
):
    other_refs, scratch = rest[:side * side - 1], rest[side * side - 1:]
    (
        total_ref, pick_rows, mine, given, got, raw, apart, w_down, w_in, partial, sums, terms,
        load_sem, sum_send, sum_recv, term_send, term_recv, out_sem, pair_send, pair_recv,
    ) = scratch
    z, column = lax.axis_index("row"), lax.axis_index("col")
    core, chip = lax.rem(column, 2), column // 2
    mate = {"col": chip * 2 + 1 - core}
    shifts = [(dy, dx) for dy in range(side) for dx in range(side)]
    middle = size // 2
    slots = w_down.shape[0]
    held = partial.shape[0]
    near = jnp.minimum(z, size - 1 - z)
    count = partial.shape[1]
    cut = count // 16 * 8
    spans = (slice(0, cut), slice(cut, count))

    def owner_of(u):
        return middle - 1 + lax.rem(u, 2)

    def loads(u):
        columns = pl.ds(pl.multiple_of(u * wide, wide), wide)
        slot = lax.rem(u, 2)
        return (
            pltpu.make_async_copy(in_ref.at[:, :, columns], raw.at[slot], load_sem.at[0, slot]),
            pltpu.make_async_copy(down_ref.at[columns, :], w_down.at[lax.rem(u, slots)], load_sem.at[1, slot]),
        )

    def sum_copy(u, side, h):
        return pltpu.make_async_remote_copy(
            src_ref=sums.at[side, u, spans[h]], dst_ref=sums.at[side, u, spans[h]],
            send_sem=sum_send.at[h, u], recv_sem=sum_recv.at[h, side, u],
            device_id={"row": z + 1 - 2 * side}, device_id_type=MESH,
        )

    def term_copy(u, side, h):
        return pltpu.make_async_remote_copy(
            src_ref=terms.at[u, spans[h]], dst_ref=terms.at[u, spans[h]],
            send_sem=term_send.at[h, side, u], recv_sem=term_recv.at[h, u],
            device_id={"row": z + 1 - 2 * side}, device_id_type=MESH,
        )

    def out_copies(u):
        columns = pl.ds(pl.multiple_of(u * wide, wide), wide)
        return [
            pltpu.make_async_copy(
                terms.at[u, :, k * wide:(k + 1) * wide], ref.at[:, columns], out_sem.at[k, u]
            )
            for k, ref in enumerate((hidden_ref, d_gate_ref, d_up_ref))
        ]

    barrier = pltpu.get_barrier_semaphore()
    for step in (-1, 1):
        @pl.when((z + step >= 0) & (z + step < size))
        def _():
            pl.semaphore_signal(barrier, inc=1, device_id={"row": z + step}, device_id_type=MESH)
    pl.semaphore_signal(barrier, inc=1, device_id=mate, device_id_type=MESH)
    for copy in loads(0):
        copy.start()
    @pl.loop(0, count // 8)
    def _(step):
        total_ref[pl.ds(pl.multiple_of(step * 8, 8), 8), :] = jnp.zeros((8, total_ref.shape[1]), jnp.float32)

    depth = down_ref.shape[1]
    rows = own_ref.shape[0]
    same = lax.broadcasted_iota(jnp.int32, (count, count), 0) == lax.broadcasted_iota(jnp.int32, (count, count), 1)
    turned = dot(pick_ref[:count], same.astype(jnp.float32).astype(jnp.bfloat16), OVER_FIRST)
    pick_rows[...] = turned.astype(jnp.bfloat16)
    pl.semaphore_wait(barrier, jnp.where(near > 0, 3, 2))

    @pl.loop(0, units + 2 * middle + 3)
    def _(t):
        @pl.when(t < units)
        def _():
            for copy in loads(t):
                copy.wait()

            @pl.when(t + 1 < units)
            def _():
                for copy in loads(t + 1):
                    copy.start()

            slot, here = lax.rem(t, slots), lax.rem(t, held)
            unpack(raw.at[lax.rem(t, 2)], w_in.at[slot], apart)
            partial[here, :, :2 * wide] = dot(packed_ref[0, :count], w_in[slot])
            partial[here, :, 2 * wide:] = dot(packed_ref[1, :count], w_down[slot], OVER_LAST)

        relayed = t - near

        @pl.when((relayed >= 0) & (relayed < units) & (owner_of(relayed) != z))
        def _():
            side = jnp.where(z < owner_of(relayed), 0, 1)
            here = lax.rem(relayed, held)
            for h, span in enumerate(spans):
                @pl.when(near > 0)
                def _():
                    sum_copy(relayed, side, h).wait_recv()
                    sums[side, relayed, span] = (
                        partial[here, span] + sums[side, relayed, span].astype(jnp.float32)
                    ).astype(sums.dtype)

                @pl.when(near == 0)
                def _():
                    sums[side, relayed, span] = partial[here, span].astype(sums.dtype)

                sum_copy(relayed, side, h).start()

        closed = t - middle

        @pl.when((closed >= 0) & (closed < units) & (owner_of(closed) == z))
        def _():
            here = lax.rem(closed, held)
            for h, span in enumerate(spans):
                @pl.when(z > 0)
                def _():
                    sum_copy(closed, 0, h).wait_recv()
                    partial[here, span] += sums[0, closed, span].astype(jnp.float32)

                @pl.when(z < size - 1)
                def _():
                    sum_copy(closed, 1, h).wait_recv()
                    partial[here, span] += sums[1, closed, span].astype(jnp.float32)

                results = swiglu_terms(*(partial[here, span, k * wide:(k + 1) * wide] for k in range(3)))
                for k, result in enumerate(results):
                    terms[closed, span, k * wide:(k + 1) * wide] = result.astype(jnp.bfloat16)

                @pl.when(z < size - 1)
                def _():
                    term_copy(closed, 0, h).start()

                @pl.when(z > 0)
                def _():
                    term_copy(closed, 1, h).start()

        passed = t - (2 * middle + 2 - near)

        @pl.when((passed >= 0) & (passed < units) & (owner_of(passed) != z) & (near > 0))
        def _():
            side = jnp.where(z < owner_of(passed), 1, 0)
            for h in range(2):
                term_copy(passed, side, h).wait_recv()
                term_copy(passed, side, h).start()

        used = t - (2 * middle + 3 - near)

        @pl.when((used >= 0) & (used < units))
        def _():
            @pl.when((owner_of(used) != z) & (near == 0))
            def _():
                for h in range(2):
                    term_copy(used, 0, h).wait_recv()

            for copy in out_copies(used):
                copy.start()
            slot = lax.rem(used, slots)
            total_ref[:, :depth] += dot(terms[used, :, :wide], w_down[slot])
            total_ref[:, depth:] += dot(terms[used, :, wide:], w_in[slot], OVER_LAST)

    span = mine.shape[2]

    def pair_copy(b):
        return pltpu.make_async_remote_copy(
            src_ref=given.at[b], dst_ref=got.at[b], send_sem=pair_send.at[b], recv_sem=pair_recv.at[b],
            device_id=mate, device_id_type=MESH,
        )

    def chosen_rows(which):
        parts = []
        for dy, dx in shifts:
            there = lax.rem(chip // side + dy, side) * side + lax.rem(lax.rem(chip, side) + dx, side)
            start = pl.multiple_of((there * 2 + which) * rows, rows)
            parts.append(pick_rows[pl.ds(start, rows), :])
        return jnp.concatenate(parts, axis=0)

    ours, theirs = chosen_rows(core), chosen_rows(1 - core)

    @pl.loop(0, mine.shape[0])
    def _(b):
        part = total_ref[:, pl.ds(pl.multiple_of(b * span, span), span)]
        high = part.astype(jnp.bfloat16)
        low = (part - high.astype(jnp.float32)).astype(jnp.bfloat16)
        given[b] = (dot(theirs, high) + dot(theirs, low)).astype(jnp.bfloat16)
        pair_copy(b).start()
        mine[b] = dot(ours, high) + dot(ours, low)

    @pl.loop(0, mine.shape[0])
    def _(b):
        pair_copy(b).wait_recv()
        columns = pl.ds(pl.multiple_of(b * span, span), span)
        both = mine[b] + got[b].astype(jnp.float32)
        for k, ref in enumerate((own_ref,) + tuple(other_refs)):
            ref[:, columns] = both[k * rows:(k + 1) * rows].astype(ref.dtype)

    @pl.loop(0, mine.shape[0])
    def _(b):
        pair_copy(b).wait_send()

    @pl.loop(0, units)
    def _(u):
        owner = owner_of(u)
        for copy in out_copies(u):
            copy.wait()

        @pl.when(owner != z)
        def _():
            for h in range(2):
                sum_copy(u, jnp.where(z < owner, 0, 1), h).wait_send()

            @pl.when(near > 0)
            def _():
                for h in range(2):
                    term_copy(u, jnp.where(z < owner, 1, 0), h).wait_send()

        @pl.when(owner == z)
        def _():
            @pl.when(z < size - 1)
            def _():
                for h in range(2):
                    term_copy(u, 0, h).wait_send()

            @pl.when(z > 0)
            def _():
                for h in range(2):
                    term_copy(u, 1, h).wait_send()


def chain(packed, pick, count, in_weight, down_weight, collective_id):
    size, columns = lax.axis_size("row"), lax.axis_size("col")
    side = math.isqrt(columns // 2)
    chips, rows = side * side, pick.shape[1] // columns
    blocks = 8
    depth = packed.shape[2]
    width = down_weight.shape[0]
    wide = 128
    units = width // wide
    slots = 2 * (size // 2) + 6
    held = size // 2 + 1
    sum_type = jnp.bfloat16 if size <= 4 else jnp.float32
    vmem, hbm = pl.BlockSpec(memory_space=pltpu.VMEM), pl.BlockSpec(memory_space=pl.ANY)
    dma = pltpu.SemaphoreType.DMA
    return pl.pallas_call(
        functools.partial(chain_kernel, size, side, units, wide),
        in_specs=[vmem, vmem, hbm, hbm],
        out_specs=[hbm] * 3 + [vmem] * chips,
        out_shape=[jax.ShapeDtypeStruct((count, width), jnp.bfloat16)] * 3
        + [jax.ShapeDtypeStruct((rows, 2 * depth), jnp.float32)]
        + [jax.ShapeDtypeStruct((rows, 2 * depth), jnp.bfloat16)] * (chips - 1),
        scratch_shapes=[
            pltpu.VMEM((count, 2 * depth), jnp.float32),
            pltpu.VMEM((pick.shape[1], count), jnp.bfloat16),
            pltpu.VMEM((blocks, chips * rows, 2 * depth // blocks), jnp.float32),
            pltpu.VMEM((blocks, chips * rows, 2 * depth // blocks), jnp.bfloat16),
            pltpu.VMEM((blocks, chips * rows, 2 * depth // blocks), jnp.bfloat16),
            pltpu.VMEM((2, depth, 2, wide), jnp.bfloat16),
            pltpu.VMEM((8, 128, wide), jnp.float32),
            pltpu.VMEM((slots, wide, depth), jnp.bfloat16),
            pltpu.VMEM((slots, depth, 2 * wide), jnp.bfloat16),
            pltpu.VMEM((held, count, 3 * wide), jnp.float32),
            pltpu.VMEM((2, units, count, 3 * wide), sum_type),
            pltpu.VMEM((units, count, 3 * wide), jnp.bfloat16),
            dma((2, 2)), dma((2, units)), dma((2, 2, units)), dma((2, 2, units)), dma((2, units)), dma((3, units)),
            dma((blocks,)), dma((blocks,)),
        ],
        compiler_params=pltpu.CompilerParams(
            collective_id=collective_id, has_side_effects=True, vmem_limit_bytes=60 * 1024 * 1024
        ),
        cost_estimate=pl.CostEstimate(
            flops=12 * count * depth * width, bytes_accessed=6 * depth * width, transcendentals=count * width
        ),
    )(packed, pick, in_weight, down_weight)


def per_device(tokens, modality, in_weight, down_weight, d_mixed):
    total = tokens.shape[0] * lax.axis_size("col")
    depth = tokens.shape[1]
    rooms = (total // 2, total * 9 // 16)
    packed, pick, count = gather_packed(tokens, modality, d_mixed, rooms[-1], 1)

    def gradients(packed, hidden, d_gate, d_up, blocks, widest):
        mine = chip_sum(blocks).astype(jnp.bfloat16)
        d_down = dot(hidden, packed[1, :hidden.shape[0]], OVER_FIRST).astype(jnp.bfloat16)
        return (mine[:, :depth], d_down, in_gradient(packed, d_gate, d_up, widest), mine[:, depth:])

    def packed_form(room, collective_id, packed, pick, tokens, modality, d_mixed, w_in, w_down):
        hidden, d_gate, d_up, *blocks = chain(packed, pick, room, w_in, w_down, collective_id)
        return gradients(packed, hidden, d_gate, d_up, blocks, 4096)

    def whole_form(packed, pick, tokens, modality, d_mixed, w_in, w_down):
        keep = (gather(modality, "row") == 1)[:, None].astype(jnp.bfloat16)
        both = gather(jnp.concatenate([tokens, d_mixed], 1), "col") * keep
        both = both.reshape(total, 2, depth).transpose(1, 0, 2)
        room = total // 2

        def half_of(k):
            part = lax.dynamic_slice_in_dim(both, k * room, room, 1)
            spots = jnp.arange(room)[:, None] + k * room == jnp.arange(total)[None, :]
            return chain(part, spots.astype(jnp.bfloat16), room, w_in, w_down, 2 + len(rooms))

        outs = lax.map(lambda k: lax.optimization_barrier(half_of(k)), jnp.arange(2))
        hidden, d_gate, d_up = (x.reshape(total, -1) for x in outs[:3])
        return gradients(both, hidden, d_gate, d_up, [x[0] + x[1] for x in outs[3:]], 512)

    forms = [functools.partial(packed_form, room, 2 + k) for k, room in enumerate(rooms)] + [whole_form]
    chosen = sum((count[0, 0] > room).astype(jnp.int32) for room in rooms)
    return lax.switch(chosen, forms, packed, pick, tokens, modality, d_mixed, in_weight, down_weight)


def solution(mesh):
    return jax.shard_map(
        per_device,
        mesh=mesh,
        in_specs=(
            P("col", "row"),
            P("row"),
            P("row", None, "col"),
            P("col", "row"),
            P("col", "row"),
        ),
        out_specs=(P("col", "row"), P("col", "row"), P("row", None, "col"), P("col", "row")),
        check_vma=False,
    )
```
